512 devices in a mesh: dp: 128 (over z_lo, y, x, core), tensor: 4 (over z_hi).
Axes of the slice: x: 4, y: 4, z: 16 (z_hi: 4, z_lo: 4; z = z_hi * 4 + z_lo), core: 2. Of those that a mesh axis runs over, the one named last changes fastest.
Arguments:
- hidden_in: bfloat16 [16384, 2048], P('dp', 'tensor'), may hold values from -6 to 6
- lengths: int32 [128, 4], P('dp'), may hold values from 1 to 80, 128 in all within a row
- routes: int32 [16384, 6], P('dp'), may hold values from 0 to 63, all different within a row; in each aligned block of 128 rows (0 to 127, 128 to 255, ...) at most 14 rows name the same one
- gate_weights: bfloat16 [16384, 6], P('dp'), may hold values from 0.099609375 to 0.59765625
- norm_gain: float32 [2048], replicated, may hold values from 0.1 to 1.9
- latent_gain: float32 [512], replicated, may hold values from 0.1 to 1.9
- moe_gain: float32 [2048], replicated, may hold values from 0.1 to 1.9
- query_train: float32 [2048, 1536], P(('dp', 'tensor')), may hold values from -1 to 1
- latent_train: float32 [2048, 576], P(('dp', 'tensor')), may hold values from -1 to 1
- expand_train: float32 [512, 2048], P(('dp', 'tensor')), may hold values from -1 to 1
- output_train: float32 [2048, 1024], P(('dp', 'tensor')), may hold values from -0.1875 to 0.1875
- expert_gate: bfloat16 [128, 2048, 704], P('dp', None, 'tensor'), may hold values from -0.125 to 0.125
- expert_up: bfloat16 [128, 2048, 704], P('dp', None, 'tensor'), may hold values from -0.125 to 0.125
- expert_down: bfloat16 [128, 704, 2048], P('dp', None, 'tensor'), may hold values from -0.21875 to 0.21875
Outputs:
- hidden_out: bfloat16 [16384, 2048], P('dp', 'tensor')
- expand_server: bfloat16 [512, 2048], P(None, 'tensor')
- output_server: bfloat16 [2048, 1024], P(None, 'tensor')
- latent_cache: bfloat16 [16384, 576], P('dp', 'tensor')
The draws below stay inside these ranges and needn't reach their ends.
Inputs may be any that keep to these rules, and one draw needn't show every extreme that they name: `lengths`: the prompts of each data group fill its 128 tokens; in every draw some prompt has exactly 80 tokens. `routes`: A token names 6 different experts; within the 128 rows of one data group no expert is named by more than 14 tokens, and in every draw some expert is named by exactly 14.
All inputs are finite; a program needn't handle non-finite values.
Results may differ from the reference program's by a relative error of at most 0.02.
Values may be sent and summed in bfloat16 or wider, within the bound.
No kernel may reach another device: no remote copies, remote signals or barrier semaphores. Data moves between devices by JAX's collectives and lax.ppermute only.
A program may use at most 64 MiB of HBM per device.

```python
import math
import jax
import jax.numpy as jnp
import numpy as np
from jax import lax

D = 2048
HEADS = 8
NOPE = 128
ROPE = 64
VDIM = 128
LATENT = 512
EXPERTS = 64
TOPK = 6
FFH = 704
PROMPTS = 4
TOK_DEV = 128
CAP = 14
MOST = 80
SUBS = 128
TOKENS = 16384
N_DP = 128


def draw_hidden_in(key, part):
    noise_part = jax.random.truncated_normal(jax.random.fold_in(key, 1), -6.0, 6.0, (TOKENS, D), jnp.float32)
    return noise_part.astype(jnp.bfloat16)


def draw_query_train(key, part):
    base_part = jax.random.truncated_normal(jax.random.fold_in(key, 11), -4.0, 4.0, (D, HEADS * (NOPE + ROPE)), jnp.float32) / math.sqrt(D)
    return base_part


def draw_latent_train(key, part):
    base_part = jax.random.truncated_normal(jax.random.fold_in(key, 12), -4.0, 4.0, (D, LATENT + ROPE), jnp.float32) / math.sqrt(D)
    return base_part


def draw_expand_train(key, part):
    base_part = jax.random.truncated_normal(jax.random.fold_in(key, 13), -4.0, 4.0, (LATENT, HEADS * (NOPE + VDIM)), jnp.float32) / math.sqrt(LATENT)
    return base_part


def level_of(stream_key, shape, shards, smallest, high):
    gain = 1.0
    for dim, blocks in shards:
        steps = jax.random.uniform(jax.random.fold_in(jax.random.fold_in(stream_key, 6), dim), (blocks,), jnp.float32, smallest / len(shards), high / len(shards))
        gain = gain * jnp.repeat(jnp.exp(steps), shape[dim] // blocks).reshape((-1,) + (1,) * (len(shape) - 1 - dim))
    return gain


def length_profile(amount, total, reach, lean):
    weights = [(1 << 20) // math.isqrt(rank ** lean) + 1 for rank in range(2, amount + 1)]
    spare, holding = total - reach - (amount - 1), [1] * (amount - 1)
    while spare > 0:
        free = [i for i in range(amount - 1) if holding[i] < reach]
        mass, budget = sum([weights[i] for i in free]), spare
        for i in free:
            extra = min(reach - holding[i], max(1, budget * weights[i] // mass), spare)
            holding[i] = holding[i] + extra
            spare = spare - extra
    return np.array([reach] + holding)


def uneven(rng, count, total, most, skew):
    if count == 2:
        one = jax.random.randint(rng, (), max(1, total - most), min(most, total - 1) + 1)
        return jnp.stack([one, total - one])
    sizes = jnp.asarray(length_profile(count, total, most, skew), jnp.int32)
    couples = (count - 1) // 2
    source_of, receiver = sizes[1:1 + 2 * couples:2], sizes[2:2 + 2 * couples:2]
    slack = jnp.minimum(source_of - 1, most - receiver)
    shifted = jax.random.randint(jax.random.fold_in(rng, 1), (couples,), 0, 1 << 20) % (slack + 1)
    sizes = sizes.at[1:1 + 2 * couples:2].set(source_of - shifted).at[2:2 + 2 * couples:2].set(receiver + shifted)
    return sizes[jax.random.permutation(jax.random.fold_in(rng, 2), count)]


def shared_out(stream_key, own, number, rows, number_of, top, bound, skew):
    sequence = jax.random.permutation(stream_key, number_of)
    packed, ordinary = load_shares(number_of, rows * top, bound, skew, True), load_shares(number_of, rows * top, bound, skew, False)
    places = jnp.arange(number_of)

    def named(sizes, turn):
        used = int((sizes > 0).sum())
        fixed = max(1, used // 4)
        shifted = fixed + (places - fixed + turn * (used - fixed)) % max(1, number_of - fixed)
        return jnp.zeros((number_of,), jnp.int32).at[sequence[jnp.where(places < fixed, places, shifted)]].set(jnp.asarray(sizes, jnp.int32))

    sizes = jnp.where(number % 4 == 0, named(packed, number // 4), named(ordinary, number - number // 4 - 1))
    mixed = jax.random.permutation(jax.random.fold_in(own, 3), number_of)
    giver, receiver = mixed[0:number_of // 2 * 2:2], mixed[1:number_of // 2 * 2:2]
    room = jnp.minimum(sizes[giver] - 1, bound - sizes[receiver]) // 2
    room = jnp.where((giver == sequence[0]) | (receiver == sequence[0]) | (sizes[receiver] == 0), 0, jnp.maximum(room, 0))
    shifted = jax.random.randint(jax.random.fold_in(own, 4), (number_of // 2,), 0, 1 << 20) % (room + 1)
    sizes = sizes.at[giver].add(-shifted).at[receiver].add(shifted)
    members = jnp.searchsorted(jnp.cumsum(sizes), jnp.arange(rows * top), side="right").astype(jnp.int32)
    table = members.reshape(top, rows).T
    table = table[jax.random.permutation(jax.random.fold_in(own, 1), rows)]
    turn = jax.random.randint(jax.random.fold_in(own, 2), (rows, 1), 0, top)
    return jnp.take_along_axis(table, (jnp.arange(top)[None, :] + turn) % top, axis=1)


def load_shares(count, total, reach, lean, full):
    weights = [(1 << 20) // math.isqrt(standing ** lean) + 1 for standing in range(1, count + 1)]
    largest = reach if full else min(reach, max(-(-total // count), total * weights[0] // sum(weights)))
    least = 1 if total - largest >= count - 1 else 0
    holding, spare = [largest] + [least] * (count - 1), total - largest - least * (count - 1)
    while spare > 0:
        candidates = [i for i in range(1, count) if holding[i] < largest] or [i for i in range(1, count) if holding[i] < reach]
        whole, remaining = sum([weights[i] for i in candidates]), spare
        for i in candidates:
            extra = min(reach - holding[i], max(1, remaining * weights[i] // whole), spare)
            holding[i] = holding[i] + extra
            spare = spare - extra
    return np.array(holding)


def normal_values(key, dims, spread, reach, split=(), kind=jnp.bfloat16):
    entries = spread * jax.random.normal(key, dims, jnp.float32)
    if split:
        entries = entries * level_of(key, dims, split, -0.22, 0.18)
    return jnp.clip(entries, -reach, reach).astype(kind)


def setup_inputs(seed: int = 0) -> dict:
    keys = jax.random.split(jax.random.key(seed), 15)
    hidden_in = draw_hidden_in(jax.random.fold_in(keys[14], 71), 0)
    lengths = jax.vmap(lambda own: uneven(own, PROMPTS, TOK_DEV, MOST, 2))(jax.random.split(keys[1], N_DP)).reshape((N_DP, PROMPTS)).astype(jnp.int32)
    routes_keys = jax.random.split(jax.random.fold_in(keys[2], 1), TOKENS // TOK_DEV)
    routes_turns = jax.random.permutation(jax.random.fold_in(keys[2], 3), TOKENS // TOK_DEV)
    routes = jax.vmap(lambda own, number: shared_out(jax.random.fold_in(keys[2], 2), own, number, TOK_DEV, EXPERTS, TOPK, CAP, 2))(routes_keys, routes_turns).reshape((TOKENS, TOPK))
    gate_weights = jnp.clip(0.099609375 + 0.49804688 * jax.random.uniform(keys[3], (TOKENS, TOPK), jnp.float32) ** level_of(keys[3], (TOKENS, TOPK), ((0, 128),), -0.2, 0.2), 0.099609375, 0.59765625).astype(jnp.bfloat16)
    norm_gain = jnp.clip(1.0 + 0.18 * jax.random.normal(keys[4], (D,), jnp.float32), 0.1, 1.9)
    latent_gain = jnp.clip(1.0 + 0.18 * jax.random.normal(keys[5], (LATENT,), jnp.float32), 0.1, 1.9)
    moe_gain = jnp.clip(1.0 + 0.18 * jax.random.normal(keys[6], (D,), jnp.float32), 0.1, 1.9)
    query_train = draw_query_train(jax.random.fold_in(keys[14], 71), 0)
    latent_train = draw_latent_train(jax.random.fold_in(keys[14], 71), 0)
    expand_train = draw_expand_train(jax.random.fold_in(keys[14], 71), 0)
    output_train = normal_values(keys[10], (D, HEADS * VDIM), (HEADS * VDIM) ** -0.5, 0.1875, ((0, 512),), jnp.float32)
    expert_gate = normal_values(keys[11], (SUBS, D, FFH), D ** -0.5, 0.125, ((0, 128), (2, 4)))
    expert_up = normal_values(keys[12], (SUBS, D, FFH), D ** -0.5, 0.125, ((0, 128), (2, 4)))
    expert_down = normal_values(keys[13], (SUBS, FFH, D), FFH ** -0.5, 0.21875, ((0, 128), (2, 4)))
    return {"hidden_in": hidden_in, "lengths": lengths, "routes": routes, "gate_weights": gate_weights, "norm_gain": norm_gain, "latent_gain": latent_gain, "moe_gain": moe_gain, "query_train": query_train, "latent_train": latent_train, "expand_train": expand_train, "output_train": output_train, "expert_gate": expert_gate, "expert_up": expert_up, "expert_down": expert_down}


rope_base = 50000.0

def rms_norm(values, gain_vector):
    mean_square = lax.optimization_barrier(jnp.mean(values * values, axis=-1, keepdims=True))
    return values * lax.rsqrt(mean_square + 1e-06) * gain_vector

def rotate(values, positions):
    half_width = values.shape[-1] // 2
    frequency = jnp.exp(jnp.arange(half_width, dtype=jnp.float32) * (-2.0 * math.log(rope_base) / values.shape[-1]))
    angles = positions.astype(jnp.float32)[:, None] * frequency[None, :]
    if values.ndim == 3:
        angles = angles[:, None, :]
    cosine = jnp.cos(angles)
    sine = jnp.sin(angles)
    first_half = values[..., :half_width]
    second_half = values[..., half_width:]
    return jnp.concatenate([first_half * cosine - second_half * sine, second_half * cosine + first_half * sine], axis=-1)

def positions_of(lengths, row_count):
    prompt_ends = jnp.cumsum(lengths, axis=1).astype(jnp.int32)
    starts = prompt_ends - lengths
    token_index = jnp.arange(row_count, dtype=jnp.int32)
    segment = lax.optimization_barrier(jnp.sum((token_index[None, :, None] >= prompt_ends[:, None, :]).astype(jnp.int32), axis=2))
    member = segment[:, :, None] == jnp.arange(lengths.shape[1], dtype=jnp.int32)[None, None, :]
    offset = lax.optimization_barrier(jnp.sum(jnp.where(member, starts[:, None, :], 0), axis=2)).astype(jnp.int32)
    return (segment, token_index[None, :] - offset)

def expert_ranks(route_groups):
    onehot = (route_groups[..., None] == jnp.arange(EXPERTS, dtype=jnp.int32)).astype(jnp.int32)
    per_token = lax.optimization_barrier(jnp.sum(onehot, axis=2))
    before = jnp.cumsum(per_token, axis=1) - per_token
    return lax.optimization_barrier(jnp.sum(onehot * before[:, :, None, :], axis=3)).astype(jnp.int32)

def attend_group(group):
    query_nope, query_rope, key_nope, key_rope, value_part, segment = group
    row_count = segment.shape[0]
    scores = jnp.einsum('qhd,khd->hqk', query_nope.astype(jnp.float32), key_nope.astype(jnp.float32))
    scores = scores + jnp.einsum('qhd,kd->hqk', query_rope.astype(jnp.float32), key_rope.astype(jnp.float32))
    scores = scores * (1.0 / math.sqrt(NOPE + ROPE))
    token_index = jnp.arange(row_count, dtype=jnp.int32)
    allowed = (segment[:, None] == segment[None, :]) & (token_index[None, :] <= token_index[:, None])
    scores = jnp.where(allowed[None], scores, -1e+30)
    largest = lax.optimization_barrier(jnp.max(scores, axis=-1, keepdims=True))
    powers = jnp.exp(scores - largest)
    probs = (powers / lax.optimization_barrier(jnp.sum(powers, axis=-1, keepdims=True))).astype(jnp.bfloat16)
    attended = jnp.einsum('hqk,khd->qhd', probs.astype(jnp.float32), value_part.astype(jnp.float32))
    return attended.astype(jnp.bfloat16).reshape(row_count, -1)

def run_expert(operands):
    token_rows, gate_pair, up_pair, down_pair = operands
    summed = jnp.zeros((token_rows.shape[0], D), jnp.float32)
    for half_index in range(2):
        gate_part = jnp.dot(token_rows, gate_pair[half_index], preferred_element_type=jnp.float32)
        up_part = jnp.dot(token_rows, up_pair[half_index], preferred_element_type=jnp.float32)
        hidden_part = (jax.nn.silu(gate_part) * up_part).astype(jnp.bfloat16)
        half_out = jnp.dot(hidden_part, down_pair[half_index], preferred_element_type=jnp.float32).astype(jnp.bfloat16)
        half_out = lax.optimization_barrier(half_out)
        summed = summed + half_out.astype(jnp.float32)
    return summed

def reference(hidden_in, lengths, routes, gate_weights, norm_gain, latent_gain, moe_gain, query_train, latent_train, expand_train, output_train, expert_gate, expert_up, expert_down):
    query_server = query_train.astype(jnp.bfloat16)
    latent_server = latent_train.astype(jnp.bfloat16)
    expand_server = expand_train.astype(jnp.bfloat16)
    output_server = output_train.astype(jnp.bfloat16)
    residual = hidden_in.astype(jnp.float32)
    normed = rms_norm(residual, norm_gain).astype(jnp.bfloat16)
    query = jnp.dot(normed, query_server, preferred_element_type=jnp.float32).reshape(TOKENS, HEADS, NOPE + ROPE)
    compressed = jnp.dot(normed, latent_server, preferred_element_type=jnp.float32).astype(jnp.bfloat16)
    segment, position = positions_of(lengths, TOK_DEV)
    segment = segment.reshape(TOKENS)
    position = position.reshape(TOKENS)
    latent_normed = rms_norm(compressed[:, :LATENT].astype(jnp.float32), latent_gain).astype(jnp.bfloat16)
    key_rope = rotate(compressed[:, LATENT:].astype(jnp.float32), position).astype(jnp.bfloat16)
    latent_cache = jnp.concatenate([latent_normed, key_rope], axis=1)
    expanded = jnp.dot(latent_normed, expand_server, preferred_element_type=jnp.float32).astype(jnp.bfloat16)
    expanded = expanded.reshape(TOKENS, HEADS, NOPE + VDIM)
    query_nope = query[..., :NOPE].astype(jnp.bfloat16)
    query_rope = rotate(query[..., NOPE:], position).astype(jnp.bfloat16)
    grouped = (query_nope.reshape(N_DP, TOK_DEV, HEADS, NOPE), query_rope.reshape(N_DP, TOK_DEV, HEADS, ROPE), expanded[..., :NOPE].reshape(N_DP, TOK_DEV, HEADS, NOPE), key_rope.reshape(N_DP, TOK_DEV, ROPE), expanded[..., NOPE:].reshape(N_DP, TOK_DEV, HEADS, VDIM), segment.reshape(N_DP, TOK_DEV))
    attended = lax.map(attend_group, grouped).reshape(TOKENS, HEADS * VDIM)
    mixed_sum = residual + jnp.dot(attended, output_server.T, preferred_element_type=jnp.float32)
    mixed = mixed_sum.astype(jnp.bfloat16)
    moe_in = rms_norm(mixed.astype(jnp.float32), moe_gain).astype(jnp.bfloat16)
    route_groups = routes.reshape(N_DP, TOK_DEV, TOPK)
    slot_rank = expert_ranks(route_groups)
    group_ids = jnp.arange(N_DP, dtype=jnp.int32)[:, None, None]
    flat_slot = ((route_groups * N_DP + group_ids) * CAP + slot_rank).reshape(-1).astype(jnp.int32)
    buffer = jnp.zeros((EXPERTS * N_DP * CAP, D), jnp.bfloat16).at[flat_slot].set(jnp.repeat(moe_in, TOPK, axis=0))
    buffer = buffer.reshape(EXPERTS, N_DP * CAP, D)
    summed = lax.map(run_expert, (buffer, expert_gate.reshape(EXPERTS, 2, D, FFH), expert_up.reshape(EXPERTS, 2, D, FFH), expert_down.reshape(EXPERTS, 2, FFH, D)))
    picked = summed.reshape(EXPERTS * N_DP * CAP, D)[flat_slot].reshape(TOKENS, TOPK, D)
    expert_sum = lax.optimization_barrier(jnp.sum(picked * gate_weights.astype(jnp.float32)[:, :, None], axis=1))
    hidden_out = (mixed.astype(jnp.float32) + expert_sum).astype(jnp.bfloat16)
    return (hidden_out, expand_server, output_server, latent_cache)
```

```python
import math

import jax
import jax.numpy as jnp
from jax import lax
from jax.experimental import pallas as pl
from jax.experimental.pallas import tpu as pltpu
from jax.sharding import Mesh
from jax.sharding import PartitionSpec as P

D = 2048
NOPE = 128
ROPE = 64
VDIM = 128
LATENT = 512
EXPERTS = 64
CAP = 14
TOK = 128
CHUNKS = 2
SLOTS = CAP // CHUNKS
ROWS = 8

DP = ("zl", "y", "x", "c")
T = "t"
BF = jnp.bfloat16
F32 = jnp.float32

QW = 384
EW = 128
LW = 576
OW = 1024
SET1 = QW + EW + LW

rope_base = 50000.0


def rms_norm(values, gain_vector):
    mean_square = jnp.mean(values * values, axis=-1, keepdims=True)
    return values * lax.rsqrt(mean_square + 1e-06) * gain_vector


def rotate(values, positions):
    half_width = values.shape[-1] // 2
    frequency = jnp.exp(
        jnp.arange(half_width, dtype=F32) * (-2.0 * math.log(rope_base) / values.shape[-1])
    )
    angles = positions.astype(F32)[:, None] * frequency[None, :]
    if values.ndim == 3:
        angles = angles[:, None, :]
    cosine = jnp.cos(angles)
    sine = jnp.sin(angles)
    first_half = values[..., :half_width]
    second_half = values[..., half_width:]
    return jnp.concatenate(
        [first_half * cosine - second_half * sine, second_half * cosine + first_half * sine],
        axis=-1,
    )


def positions_of(lengths, row_count):
    prompt_ends = jnp.cumsum(lengths, axis=1)
    starts = prompt_ends - lengths
    token_index = jnp.arange(row_count, dtype=jnp.int32)
    segment = jnp.sum(
        (token_index[None, :, None] >= prompt_ends[:, None, :]).astype(jnp.int32), axis=2
    )
    member = segment[:, :, None] == jnp.arange(lengths.shape[1], dtype=jnp.int32)[None, None, :]
    offset = jnp.sum(jnp.where(member, starts[:, None, :], 0), axis=2)
    return (segment, token_index[None, :] - offset)


def expert_ranks(routes):
    onehot = (routes[..., None] == jnp.arange(EXPERTS, dtype=jnp.int32)).astype(BF)
    per_token = jnp.sum(onehot, axis=1)
    index = jnp.arange(TOK, dtype=jnp.int32)
    earlier = (index[None, :] < index[:, None]).astype(BF)
    before = jnp.dot(earlier, per_token, preferred_element_type=F32)
    return jnp.sum(onehot.astype(F32) * before[:, None, :], axis=2).astype(jnp.int32)


def shifted(block, axis):
    return [block] + [
        lax.ppermute(block, axis, [(j, (j + s) % 4) for j in range(4)]) for s in range(1, 4)
    ]


def other_core(block):
    return lax.ppermute(block, "c", [(0, 1), (1, 0)])


def ordered(place, mine, theirs, widths):
    total = sum(widths)

    def kernel(place_ref, mine_ref, theirs_ref, *out_refs):
        zl, y, x, c = place_ref[0], place_ref[1], place_ref[2], place_ref[3]

        def step(i, carry):
            row_zl, row_y, row_x = i // 16, (i // 4) % 4, i % 4
            source = ((x - row_x + 4) % 4 * 4 + (y - row_y + 4) % 4) * 4 + (zl - row_zl + 4) % 4
            for ref, core in ((mine_ref, c), (theirs_ref, 1 - c)):
                at = 0
                for out_ref, width in zip(out_refs, widths):
                    out_ref[i * 2 + core] = ref[source, :, at : at + width]
                    at += width
            return carry

        lax.fori_loop(0, 64, step, 0)

    vmem = pl.BlockSpec(memory_space=pltpu.VMEM)
    outs = pl.pallas_call(
        kernel,
        out_shape=[jax.ShapeDtypeStruct((128, 16, w), BF) for w in widths],
        in_specs=[pl.BlockSpec(memory_space=pltpu.SMEM), vmem, vmem],
        out_specs=[vmem for _ in widths],
        name="ordered",
    )(place, mine.reshape(64, 16, total), theirs.reshape(64, 16, total))
    return [o.reshape(2048, w) for o, w in zip(outs, widths)]


def body(
    hidden_in,
    lengths,
    routes,
    gate_weights,
    norm_gain,
    latent_gain,
    moe_gain,
    query_train,
    latent_train,
    expand_train,
    output_train,
    expert_gate,
    expert_up,
    expert_down,
):
    rank = lax.axis_index(T)
    core = lax.axis_index("c")
    place = jnp.stack([lax.axis_index(a) for a in DP]).astype(jnp.int32)

    packed = jnp.concatenate(
        [
            query_train.reshape(4, 4, QW).transpose(1, 0, 2),
            expand_train.reshape(4, 4, EW),
            jnp.broadcast_to(latent_train[None], (4, 4, LW)),
            jnp.broadcast_to(output_train[None], (4, 4, OW)),
        ],
        axis=2,
    ).astype(BF)
    packed = lax.all_to_all(packed, T, split_axis=0, concat_axis=0, tiled=True)
    packed = packed.reshape(16, SET1 + OW)
    gathered = jnp.stack(shifted(packed, "zl"))
    gathered = jnp.stack(shifted(gathered, "y"))
    first_set = gathered[..., :SET1]
    second_set = gathered[..., SET1:]
    first_parts = shifted(first_set, "x")
    hidden_gated, _ = lax.optimization_barrier((hidden_in, first_set))
    full_input = lax.all_gather(hidden_gated, T, axis=1, tiled=True)
    first_mine = jnp.stack(first_parts)
    query_block, expand_rows, latent_full = ordered(
        place, first_mine, other_core(first_mine), (QW, EW, LW)
    )
    second_gated, _ = lax.optimization_barrier((second_set, first_mine))
    second_mine = jnp.stack(shifted(second_gated, "x"))
    (output_full,) = ordered(place, second_mine, other_core(second_mine), (OW,))
    expand_block = expand_rows.reshape(LATENT, LATENT)
    output_block = lax.dynamic_slice_in_dim(output_full, rank * 256, 256, 1)

    token_count = TOK
    normed = rms_norm(full_input.astype(F32), norm_gain).astype(BF)
    query = jnp.dot(normed, query_block, preferred_element_type=F32).reshape(
        token_count, -1, NOPE + ROPE
    )
    compressed = jnp.dot(normed, latent_full, preferred_element_type=F32).astype(BF)
    segment, position = positions_of(lengths, token_count)
    segment = segment[0]
    position = position[0]
    latent_normed = rms_norm(compressed[:, :LATENT].astype(F32), latent_gain).astype(BF)
    key_rope = rotate(compressed[:, LATENT:].astype(F32), position).astype(BF)
    cache_full = jnp.concatenate([latent_normed, key_rope], axis=1)
    cache_cols = lax.dynamic_slice_in_dim(cache_full, rank * 144, 144, 1)
    expanded = jnp.dot(latent_normed, expand_block, preferred_element_type=F32).astype(BF)
    expanded = expanded.reshape(token_count, -1, NOPE + VDIM)
    query_nope = query[..., :NOPE].astype(BF)
    query_rope = rotate(query[..., NOPE:], position).astype(BF)
    scores = jnp.einsum("qhd,khd->hqk", query_nope, expanded[..., :NOPE], preferred_element_type=F32)
    scores = scores + jnp.einsum("qhd,kd->hqk", query_rope, key_rope, preferred_element_type=F32)
    scores = scores * (1.0 / math.sqrt(NOPE + ROPE))
    token_index = jnp.arange(token_count, dtype=jnp.int32)
    allowed = (segment[:, None] == segment[None, :]) & (token_index[None, :] <= token_index[:, None])
    scores = jnp.where(allowed[None], scores, -1e30)
    largest = jnp.max(scores, axis=-1, keepdims=True)
    powers = jnp.exp(scores - largest)
    probs = (powers / jnp.sum(powers, axis=-1, keepdims=True)).astype(BF)
    attended = jnp.einsum("hqk,khd->qhd", probs, expanded[..., NOPE:], preferred_element_type=F32)
    attended = attended.astype(BF).reshape(token_count, -1)
    attended_full = lax.all_gather(attended, T, axis=1, tiled=True)
    head_total = lax.dot_general(
        attended_full, output_full, (((1,), (1,)), ((), ())), preferred_element_type=F32
    )
    mixed_full = (full_input.astype(F32) + head_total).astype(BF)
    mixed_cols = lax.dynamic_slice_in_dim(mixed_full, rank * 512, 512, 1)
    moe_in = rms_norm(mixed_full.astype(F32), moe_gain).astype(BF)

    slot_rank = expert_ranks(routes)
    row_ids = jnp.arange(EXPERTS * 2 * ROWS, dtype=jnp.int32)
    row_core = (row_ids // ROWS) % 2
    moe_halves = jnp.concatenate([moe_in[:, : D // 2], moe_in[:, D // 2 :]], axis=0)
    gates = gate_weights.astype(F32)
    compact = jnp.arange(TOK * SLOTS, dtype=jnp.int32)
    spread = (compact // SLOTS) * ROWS + compact % SLOTS
    squeeze = (jnp.arange(TOK * ROWS, dtype=jnp.int32)[:, None] == spread[None, :]).astype(BF)
    gate_mat = expert_gate[0]
    up_mat = expert_up[0]
    mine_at = core * (D // 2)
    other_at = (1 - core) * (D // 2)

    def halves(matrix):
        return (
            lax.dynamic_slice_in_dim(matrix, mine_at, D // 2, 0),
            lax.dynamic_slice_in_dim(matrix, other_at, D // 2, 0),
        )

    gate_mine, gate_other = halves(gate_mat)
    up_mine, up_other = halves(up_mat)

    def rows_by(weight, rows):
        return lax.dot_general(weight, rows, (((0,), (1,)), ((), ())), preferred_element_type=F32)

    hidden_chunks = []
    combine = []
    gate_on = None
    for k in range(CHUNKS):
        in_chunk = (slot_rank >= k * SLOTS) & (slot_rank < (k + 1) * SLOTS)
        target = jnp.where(in_chunk, routes * (2 * ROWS) + (slot_rank - k * SLOTS), -1)
        matches = (row_ids - row_core * ROWS)[:, None, None] == target[None, :, :]
        picked = jnp.sum(matches.astype(F32), axis=2)
        dispatch = jnp.concatenate(
            [
                jnp.where(row_core[:, None] == 0, picked, 0.0),
                jnp.where(row_core[:, None] == 1, picked, 0.0),
            ],
            axis=1,
        ).astype(BF)
        weighted = jnp.sum(jnp.where(matches, gates[None], 0.0), axis=2)
        combine.append(
            [jnp.where(row_core[:, None] == h, weighted, 0.0).astype(BF) for h in range(2)]
        )
        outgoing = jnp.dot(dispatch, moe_halves, preferred_element_type=F32).astype(BF)
        if gate_on is not None:
            outgoing, _ = lax.optimization_barrier((outgoing, gate_on))
        mine = lax.all_to_all(outgoing, DP, split_axis=0, concat_axis=0, tiled=True)
        theirs = other_core(mine)
        gate_part = rows_by(gate_mine, mine) + rows_by(gate_other, theirs)
        up_part = rows_by(up_mine, mine) + rows_by(up_other, theirs)
        hidden = (jax.nn.silu(gate_part) * up_part).astype(BF)
        hidden = jnp.dot(hidden, squeeze, preferred_element_type=F32).astype(BF)
        gate_on = hidden
        hidden_chunks.append(lax.all_gather(hidden, T, axis=0, tiled=True))

    result = mixed_cols.astype(F32)
    sums = [0.0, 0.0]
    for k in range(CHUNKS):
        half_out = lax.dot_general(
            hidden_chunks[k], expert_down[0], (((0,), (0,)), ((), ())), preferred_element_type=F32
        ).astype(BF)
        half_out = jnp.dot(squeeze, half_out, preferred_element_type=F32).astype(BF)
        keep = lax.dynamic_slice_in_dim(half_out, core * 256, 256, 1)
        give = lax.dynamic_slice_in_dim(half_out, (1 - core) * 256, 256, 1)
        both = (keep.astype(F32) + other_core(give).astype(F32)).astype(BF)
        returned = lax.all_to_all(both, DP, split_axis=0, concat_axis=0, tiled=True)
        for h in range(2):
            sums[h] = sums[h] + lax.dot_general(
                combine[k][h], returned, (((0,), (0,)), ((), ())), preferred_element_type=F32
            )
    hidden_out = (result + jnp.concatenate(sums, axis=1)).astype(BF)
    return (hidden_out, expand_block, output_block, cache_cols)


def solution(mesh):
    fine = Mesh(mesh.devices.reshape(4, 4, 4, 2, 4), DP + (T,))
    rows_both = P(DP + (T,), None)
    in_specs = (
        P(DP, T),
        P(DP, None),
        P(DP, None),
        P(DP, None),
        P(),
        P(),
        P(),
        rows_both,
        rows_both,
        rows_both,
        rows_both,
        P(DP, None, T),
        P(DP, None, T),
        P(DP, None, T),
    )
    out_specs = (P(DP, T), P(None, T), P(None, T), P(DP, T))
    return jax.shard_map(body, mesh=fine, in_specs=in_specs, out_specs=out_specs, check_vma=False)
```

```python
import math

import jax
import jax.numpy as jnp
from jax import lax
from jax.experimental import pallas as pl
from jax.experimental.pallas import tpu as pltpu
from jax.sharding import Mesh
from jax.sharding import PartitionSpec as P

D = 2048
NOPE = 128
ROPE = 64
VDIM = 128
LATENT = 512
EXPERTS = 64
CAP = 14
TOK = 128
PADDED = 16

DP = ("zl", "y", "x", "c")
T = "t"
BF = jnp.bfloat16
F32 = jnp.float32

QW = 384
EW = 128
LW = 576
OW = 1024
SET1 = QW + EW + LW

rope_base = 50000.0


def rms_norm(values, gain_vector):
    mean_square = jnp.mean(values * values, axis=-1, keepdims=True)
    return values * lax.rsqrt(mean_square + 1e-06) * gain_vector


def rotate(values, positions):
    half_width = values.shape[-1] // 2
    frequency = jnp.exp(
        jnp.arange(half_width, dtype=F32) * (-2.0 * math.log(rope_base) / values.shape[-1])
    )
    angles = positions.astype(F32)[:, None] * frequency[None, :]
    if values.ndim == 3:
        angles = angles[:, None, :]
    cosine = jnp.cos(angles)
    sine = jnp.sin(angles)
    first_half = values[..., :half_width]
    second_half = values[..., half_width:]
    return jnp.concatenate(
        [first_half * cosine - second_half * sine, second_half * cosine + first_half * sine],
        axis=-1,
    )


def positions_of(lengths, row_count):
    prompt_ends = jnp.cumsum(lengths, axis=1)
    starts = prompt_ends - lengths
    token_index = jnp.arange(row_count, dtype=jnp.int32)
    segment = jnp.sum(
        (token_index[None, :, None] >= prompt_ends[:, None, :]).astype(jnp.int32), axis=2
    )
    member = segment[:, :, None] == jnp.arange(lengths.shape[1], dtype=jnp.int32)[None, None, :]
    offset = jnp.sum(jnp.where(member, starts[:, None, :], 0), axis=2)
    return (segment, token_index[None, :] - offset)


def expert_ranks(routes):
    onehot = (routes[..., None] == jnp.arange(EXPERTS, dtype=jnp.int32)).astype(BF)
    per_token = jnp.sum(onehot, axis=1)
    index = jnp.arange(TOK, dtype=jnp.int32)
    earlier = (index[None, :] < index[:, None]).astype(BF)
    before = jnp.dot(earlier, per_token, preferred_element_type=F32)
    return jnp.sum(onehot.astype(F32) * before[:, None, :], axis=2).astype(jnp.int32)


def shifted(block, axis):
    return [block] + [
        lax.ppermute(block, axis, [(j, (j + s) % 4) for j in range(4)]) for s in range(1, 4)
    ]


def other_core(block):
    return lax.ppermute(block, "c", [(0, 1), (1, 0)])


def ordered(place, mine, theirs, widths):
    total = sum(widths)

    def kernel(place_ref, mine_ref, theirs_ref, *out_refs):
        zl, y, x, c = place_ref[0], place_ref[1], place_ref[2], place_ref[3]

        def step(i, carry):
            row_zl, row_y, row_x = i // 16, (i // 4) % 4, i % 4
            source = ((x - row_x + 4) % 4 * 4 + (y - row_y + 4) % 4) * 4 + (zl - row_zl + 4) % 4
            for ref, core in ((mine_ref, c), (theirs_ref, 1 - c)):
                at = 0
                for out_ref, width in zip(out_refs, widths):
                    out_ref[i * 2 + core] = ref[source, :, at : at + width]
                    at += width
            return carry

        lax.fori_loop(0, 64, step, 0)

    vmem = pl.BlockSpec(memory_space=pltpu.VMEM)
    outs = pl.pallas_call(
        kernel,
        out_shape=[jax.ShapeDtypeStruct((128, 16, w), BF) for w in widths],
        in_specs=[pl.BlockSpec(memory_space=pltpu.SMEM), vmem, vmem],
        out_specs=[vmem for _ in widths],
        name="ordered",
    )(place, mine.reshape(64, 16, total), theirs.reshape(64, 16, total))
    return [o.reshape(2048, w) for o, w in zip(outs, widths)]


def body(
    hidden_in,
    lengths,
    routes,
    gate_weights,
    norm_gain,
    latent_gain,
    moe_gain,
    query_train,
    latent_train,
    expand_train,
    output_train,
    expert_gate,
    expert_up,
    expert_down,
):
    rank = lax.axis_index(T)
    core = lax.axis_index("c")
    place = jnp.stack([lax.axis_index(a) for a in DP]).astype(jnp.int32)

    packed = jnp.concatenate(
        [
            query_train.reshape(4, 4, QW).transpose(1, 0, 2),
            expand_train.reshape(4, 4, EW),
            jnp.broadcast_to(latent_train[None], (4, 4, LW)),
            jnp.broadcast_to(output_train[None], (4, 4, OW)),
        ],
        axis=2,
    ).astype(BF)
    packed = lax.all_to_all(packed, T, split_axis=0, concat_axis=0, tiled=True)
    packed = packed.reshape(16, SET1 + OW)
    gathered = jnp.stack(shifted(packed, "zl"))
    gathered = jnp.stack(shifted(gathered, "y"))
    first_set = gathered[..., :SET1]
    second_set = gathered[..., SET1:]
    first_parts = shifted(first_set, "x")
    hidden_gated, _ = lax.optimization_barrier((hidden_in, first_set))
    full_input = lax.all_gather(hidden_gated, T, axis=1, tiled=True)
    first_mine = jnp.stack(first_parts)
    query_block, expand_rows, latent_full = ordered(
        place, first_mine, other_core(first_mine), (QW, EW, LW)
    )
    second_gated, _ = lax.optimization_barrier((second_set, first_mine))
    second_mine = jnp.stack(shifted(second_gated, "x"))
    (output_full,) = ordered(place, second_mine, other_core(second_mine), (OW,))
    expand_block = expand_rows.reshape(LATENT, LATENT)
    output_block = lax.dynamic_slice_in_dim(output_full, rank * 256, 256, 1)

    token_count = TOK
    normed = rms_norm(full_input.astype(F32), norm_gain).astype(BF)
    query = jnp.dot(normed, query_block, preferred_element_type=F32).reshape(
        token_count, -1, NOPE + ROPE
    )
    compressed = jnp.dot(normed, latent_full, preferred_element_type=F32).astype(BF)
    segment, position = positions_of(lengths, token_count)
    segment = segment[0]
    position = position[0]
    latent_normed = rms_norm(compressed[:, :LATENT].astype(F32), latent_gain).astype(BF)
    key_rope = rotate(compressed[:, LATENT:].astype(F32), position).astype(BF)
    cache_full = jnp.concatenate([latent_normed, key_rope], axis=1)
    cache_cols = lax.dynamic_slice_in_dim(cache_full, rank * 144, 144, 1)
    expanded = jnp.dot(latent_normed, expand_block, preferred_element_type=F32).astype(BF)
    expanded = expanded.reshape(token_count, -1, NOPE + VDIM)
    query_nope = query[..., :NOPE].astype(BF)
    query_rope = rotate(query[..., NOPE:], position).astype(BF)
    scores = jnp.einsum("qhd,khd->hqk", query_nope, expanded[..., :NOPE], preferred_element_type=F32)
    scores = scores + jnp.einsum("qhd,kd->hqk", query_rope, key_rope, preferred_element_type=F32)
    scores = scores * (1.0 / math.sqrt(NOPE + ROPE))
    token_index = jnp.arange(token_count, dtype=jnp.int32)
    allowed = (segment[:, None] == segment[None, :]) & (token_index[None, :] <= token_index[:, None])
    scores = jnp.where(allowed[None], scores, -1e30)
    largest = jnp.max(scores, axis=-1, keepdims=True)
    powers = jnp.exp(scores - largest)
    probs = (powers / jnp.sum(powers, axis=-1, keepdims=True)).astype(BF)
    attended = jnp.einsum("hqk,khd->qhd", probs, expanded[..., NOPE:], preferred_element_type=F32)
    attended = attended.astype(BF).reshape(token_count, -1)
    attended_full = lax.all_gather(attended, T, axis=1, tiled=True)
    head_total = lax.dot_general(
        attended_full, output_full, (((1,), (1,)), ((), ())), preferred_element_type=F32
    )
    mixed_full = (full_input.astype(F32) + head_total).astype(BF)
    mixed_cols = lax.dynamic_slice_in_dim(mixed_full, rank * 512, 512, 1)
    moe_in = rms_norm(mixed_full.astype(F32), moe_gain).astype(BF)

    slot_rank = expert_ranks(routes)
    gates = gate_weights.astype(F32)
    pad_ids = jnp.arange(EXPERTS * 2 * PADDED, dtype=jnp.int32)
    pad_core = (pad_ids // PADDED) % 2
    slot_at = routes * (2 * PADDED) + slot_rank
    matches = (pad_ids - pad_core * PADDED)[:, None, None] == slot_at[None, :, :]

    def placed_by(values):
        return jnp.sum(jnp.where(matches, values, 0.0), axis=2)

    placed = placed_by(1.0)
    dispatch = jnp.concatenate(
        [
            jnp.where(pad_core[:, None] == 0, placed, 0.0),
            jnp.where(pad_core[:, None] == 1, placed, 0.0),
        ],
        axis=1,
    ).astype(BF)
    moe_halves = jnp.concatenate([moe_in[:, : D // 2], moe_in[:, D // 2 :]], axis=0)

    weighted = placed_by(gates[None])
    combine = [jnp.where(pad_core[:, None] == h, weighted, 0.0).astype(BF) for h in range(2)]

    compact = jnp.arange(TOK * CAP, dtype=jnp.int32)
    taken = (compact // CAP) * PADDED + compact % CAP
    squeeze = (jnp.arange(TOK * PADDED, dtype=jnp.int32)[:, None] == taken[None, :]).astype(BF)

    def halves(matrix):
        return (
            lax.dynamic_slice_in_dim(matrix, core * (D // 2), D // 2, 0),
            lax.dynamic_slice_in_dim(matrix, (1 - core) * (D // 2), D // 2, 0),
        )

    gate_mine, gate_other = halves(expert_gate[0])
    up_mine, up_other = halves(expert_up[0])
    around = [(rank + 4 - back) % 4 for back in (0, 1, 3, 2)]
    down_around = jnp.concatenate(
        [lax.dynamic_slice_in_dim(expert_down[0], at * 176, 176, 0) for at in around], axis=0
    )

    def rows_by(weight, rows):
        return lax.dot_general(weight, rows, (((0,), (1,)), ((), ())), preferred_element_type=F32)

    outgoing = jnp.dot(dispatch, moe_halves, preferred_element_type=F32).astype(BF)
    mine = lax.all_to_all(outgoing, DP, split_axis=0, concat_axis=0, tiled=True)
    theirs = other_core(mine)
    gate_part = rows_by(gate_mine, mine) + rows_by(gate_other, theirs)
    up_part = rows_by(up_mine, mine) + rows_by(up_other, theirs)
    hidden = (jax.nn.silu(gate_part) * up_part).astype(BF)

    up_ring = [(j, (j + 1) % 4) for j in range(4)]
    down_ring = [(j, (j + 3) % 4) for j in range(4)]
    own = jnp.dot(hidden, squeeze, preferred_element_type=F32).astype(BF)
    below = lax.ppermute(own, T, up_ring)
    above = lax.ppermute(own, T, down_ring)
    far_first = lax.ppermute(below[:88], T, up_ring)
    far_second = lax.ppermute(above[88:], T, down_ring)

    def out_of(pieces, at):
        rows = jnp.concatenate(pieces, axis=0)
        return lax.dot_general(
            rows, down_around[at : at + rows.shape[0]], (((0,), (0,)), ((), ())),
            preferred_element_type=F32,
        )

    half_out = (out_of([own, below, above], 0) + out_of([far_first, far_second], 528)).astype(BF)
    half_out = jnp.dot(squeeze, half_out, preferred_element_type=F32).astype(BF)
    keep = lax.dynamic_slice_in_dim(half_out, core * 256, 256, 1)
    give = lax.dynamic_slice_in_dim(half_out, (1 - core) * 256, 256, 1)
    both = (keep.astype(F32) + other_core(give).astype(F32)).astype(BF)
    returned = lax.all_to_all(both, DP, split_axis=0, concat_axis=0, tiled=True)
    sums = [
        lax.dot_general(part, returned, (((0,), (0,)), ((), ())), preferred_element_type=F32)
        for part in combine
    ]
    result = mixed_cols.astype(F32)
    hidden_out = (result + jnp.concatenate(sums, axis=1)).astype(BF)
    return (hidden_out, expand_block, output_block, cache_cols)


def solution(mesh):
    fine = Mesh(mesh.devices.reshape(4, 4, 4, 2, 4), DP + (T,))
    rows_both = P(DP + (T,), None)
    in_specs = (
        P(DP, T),
        P(DP, None),
        P(DP, None),
        P(DP, None),
        P(),
        P(),
        P(),
        rows_both,
        rows_both,
        rows_both,
        rows_both,
        P(DP, None, T),
        P(DP, None, T),
        P(DP, None, T),
    )
    out_specs = (P(DP, T), P(None, T), P(None, T), P(DP, T))
    return jax.shard_map(body, mesh=fine, in_specs=in_specs, out_specs=out_specs, check_vma=False)
```

```python
import math

import jax
import jax.numpy as jnp
from jax import lax
from jax.experimental import pallas as pl
from jax.experimental.pallas import tpu as pltpu
from jax.sharding import Mesh
from jax.sharding import PartitionSpec as P

D = 2048
NOPE = 128
ROPE = 64
VDIM = 128
LATENT = 512
EXPERTS = 64
CAP = 14
TOK = 128
PADDED = 16

DP = ("zl", "y", "x", "c")
T = "t"
BF = jnp.bfloat16
F32 = jnp.float32

rope_base = 50000.0


def rms_norm(values, gain_vector):
    mean_square = jnp.mean(values * values, axis=-1, keepdims=True)
    return values * lax.rsqrt(mean_square + 1e-06) * gain_vector


def positions_of(lengths, row_count):
    prompt_ends = jnp.cumsum(lengths, axis=1)
    starts = prompt_ends - lengths
    token_index = jnp.arange(row_count, dtype=jnp.int32)
    segment = jnp.sum(
        (token_index[None, :, None] >= prompt_ends[:, None, :]).astype(jnp.int32), axis=2
    )
    member = segment[:, :, None] == jnp.arange(lengths.shape[1], dtype=jnp.int32)[None, None, :]
    offset = jnp.sum(jnp.where(member, starts[:, None, :], 0), axis=2)
    return (segment, token_index[None, :] - offset)


def expert_ranks(routes):
    onehot = (routes[..., None] == jnp.arange(EXPERTS, dtype=jnp.int32)).astype(BF)
    per_token = jnp.sum(onehot, axis=1)
    index = jnp.arange(TOK, dtype=jnp.int32)
    earlier = (index[None, :] < index[:, None]).astype(BF)
    before = jnp.dot(earlier, per_token, preferred_element_type=F32)
    return jnp.sum(onehot.astype(F32) * before[:, None, :], axis=2).astype(jnp.int32)


def shifted(block, axis):
    return [block] + [
        lax.ppermute(block, axis, [(j, (j + s) % 4) for j in range(4)]) for s in range(1, 4)
    ]


def ring(block, axis):
    half = block.shape[0] // 2
    up, down = [(j, (j + 1) % 4) for j in range(4)], [(j, (j + 3) % 4) for j in range(4)]
    below, above = lax.ppermute(block, axis, up), lax.ppermute(block, axis, down)
    far = [lax.ppermute(below[:half], axis, up), lax.ppermute(above[half:], axis, down)]
    return [block, below, jnp.concatenate(far), above]


def other_core(block):
    return lax.ppermute(block, "c", [(0, 1), (1, 0)])


VMEM = pl.BlockSpec(memory_space=pltpu.VMEM)
SMEM = pl.BlockSpec(memory_space=pltpu.SMEM)
NT = (((1,), (1,)), ((), ()))


def pack_rows(hidden_in, query, latent, expand, output):
    def kernel(hidden_ref, q_ref, l_ref, e_ref, o_ref, out_ref, rows):
        out_ref[0:128, :] = hidden_ref[...]
        tail_a, tail_b = l_ref[:, 512:544], l_ref[:, 544:576]
        tail = [tail_a, tail_a, tail_b, tail_b]
        for t in range(4):
            q = q_ref[:, t * 384 : (t + 1) * 384]
            parts = [
                q[:, 0:128], q[:, 192:320],
                q[:, 128:160], q[:, 320:352], q[:, 160:192], q[:, 352:384],
            ]
            rows[t * 4 : t * 4 + 4, :] = jnp.concatenate(parts + tail, axis=1)
            rows[20 + t : 21 + t, :] = e_ref[:, t * 512 : (t + 1) * 512]
        rows[16:20, :] = l_ref[:, 0:512]
        rows[24:28, :] = o_ref[:, 0:512]
        rows[28:32, :] = o_ref[:, 512:1024]
        out_ref[128:160, :] = rows[...].astype(BF)

    return pl.pallas_call(
        kernel,
        out_shape=jax.ShapeDtypeStruct((160, 512), BF),
        in_specs=[VMEM] * 5,
        out_specs=VMEM,
        scratch_shapes=[pltpu.VMEM((32, 512), F32)],
        name="pack_rows",
    )(hidden_in, query, latent, expand, output)


def pick_rows(place, everything):
    def kernel(place_ref, in_ref, out_ref, wide, rows):
        t = place_ref[4]
        wide[...] = in_ref[...].astype(F32)
        for s in range(4):
            lanes = slice(s * 512, (s + 1) * 512)
            q = wide[0:4, lanes]
            e = wide[20:21, lanes]
            for k in range(1, 4):
                q = jnp.where(t == k, wide[k * 4 : k * 4 + 4, lanes], q)
                e = jnp.where(t == k, wide[20 + k : 21 + k, lanes], e)
            rows[s * 4 : s * 4 + 4, :] = q
            rows[16 + s * 4 : 20 + s * 4, :] = wide[16:20, lanes]
            rows[32 + s : 33 + s, :] = e
            rows[36 + s : 37 + s, :] = e
            rows[40 + s * 4 : 44 + s * 4, :] = wide[24:28, lanes]
            rows[56 + s * 4 : 60 + s * 4, :] = wide[28:32, lanes]
        out_ref[...] = rows[...].astype(BF)

    return pl.pallas_call(
        kernel,
        grid=(1,),
        out_shape=jax.ShapeDtypeStruct((72, 512), BF),
        in_specs=[SMEM, pl.BlockSpec((32, 2048), lambda i: (4, 0))],
        out_specs=pl.BlockSpec((72, 512), lambda i: (0, 0)),
        scratch_shapes=[pltpu.VMEM((32, 2048), F32), pltpu.VMEM((72, 512), F32)],
        name="pick_rows",
    )(place, everything)


def in_order(place_ref, visit):
    zl, y, x = place_ref[0], place_ref[1], place_ref[2]

    def source_of(i):
        row_zl, row_y, row_x = i // 16, (i // 4) % 4, i % 4
        return ((x - row_x + 4) % 4 * 4 + (y - row_y + 4) % 4) * 4 + (zl - row_zl + 4) % 4

    def step(j, carry):
        visit(j, (source_of(2 * j), source_of(2 * j + 1)))
        return carry

    lax.fori_loop(0, 32, step, 0)


def attention(place, everything, mine, theirs, norm_gain, latent_gain, cosines, sines, allowed):
    def kernel(
        place_ref, in_ref, mine_ref, theirs_ref, norm_ref, gain_ref, cos_ref, sin_ref, allowed_ref,
        attended_ref, latent_ref, rope_ref, expand_ref, q_rows, l_rows,
    ):
        c = place_ref[3]
        low = lax.broadcasted_iota(jnp.int32, (8, 512), 0) < 4

        def visit(j, sources):
            pair = []
            for n, source in enumerate(sources):
                for ref, at in ((mine_ref, c), (theirs_ref, 1 - c)):
                    row = pl.multiple_of(((2 * j + n) * 2 + at) * 16, 16)
                    q_rows[pl.ds(row, 16), :] = ref[source, 0:16, :]
                    l_rows[pl.ds(row, 16), :] = ref[source, 16:32, :]
                own = mine_ref[source, 32:40, :].astype(F32)
                other = theirs_ref[source, 32:40, :].astype(F32)
                first = jnp.where(c == 0, own, other)
                second = jnp.where(c == 0, other, own)
                pair.append(jnp.where(low, first, second))
            row = pl.multiple_of(j * 16, 16)
            expand_ref[pl.ds(row, 16), :] = jnp.concatenate(pair, axis=0).astype(BF)

        in_order(place_ref, visit)
        normed = rms_norm(in_ref[...].astype(F32), norm_ref[...]).astype(BF)
        query = jnp.dot(normed, q_rows[...], preferred_element_type=F32)
        latent = jnp.dot(normed, l_rows[...], preferred_element_type=F32).astype(BF)
        latent = rms_norm(latent.astype(F32), gain_ref[...]).astype(BF)
        latent_ref[...] = latent
        cosine, sine = cos_ref[...], sin_ref[...]

        def rotated(v):
            return (v * cosine + pltpu.roll(v, 64, 1) * sine).astype(BF)

        key_rope = rotated(query[:, 384:512].astype(BF).astype(F32))
        rope_ref[...] = key_rope
        query_rope = rotated(query[:, 256:384])
        expanded = jnp.dot(latent, expand_ref[...], preferred_element_type=F32).astype(BF)
        head_of = (lax.broadcasted_iota(jnp.int32, (128, 128), 1) // 32) % 2
        for h in range(2):
            own_rope = jnp.where(head_of == h, query_rope.astype(F32), 0.0).astype(BF)
            scores = lax.dot_general(
                query[:, h * 128 : (h + 1) * 128].astype(BF),
                expanded[:, h * 256 : h * 256 + 128],
                NT,
                preferred_element_type=F32,
            )
            scores = scores + lax.dot_general(own_rope, key_rope, NT, preferred_element_type=F32)
            scores = scores * (1.0 / math.sqrt(NOPE + ROPE))
            scores = jnp.where(allowed_ref[...] > 0.0, scores, -1e30)
            powers = jnp.exp(scores - jnp.max(scores, axis=-1, keepdims=True))
            probs = (powers / jnp.sum(powers, axis=-1, keepdims=True)).astype(BF)
            out = jnp.dot(
                probs, expanded[:, h * 256 + 128 : h * 256 + 256], preferred_element_type=F32
            )
            attended_ref[:, h * 128 : (h + 1) * 128] = out.astype(BF)

    def whole(*shape):
        return pl.BlockSpec(shape, lambda i: (0,) * len(shape))

    return pl.pallas_call(
        kernel,
        grid=(1,),
        out_shape=[
            jax.ShapeDtypeStruct((128, 256), BF),
            jax.ShapeDtypeStruct((128, 512), BF),
            jax.ShapeDtypeStruct((128, 128), BF),
            jax.ShapeDtypeStruct((512, 512), BF),
        ],
        in_specs=[
            SMEM, whole(128, 2048), VMEM, VMEM,
            whole(1, 2048), whole(1, 512), whole(128, 128), whole(128, 128), whole(128, 128),
        ],
        out_specs=[whole(128, 256), whole(128, 512), whole(128, 128), whole(512, 512)],
        scratch_shapes=[pltpu.VMEM((2048, 512), BF), pltpu.VMEM((2048, 512), BF)],
        name="attention",
    )(
        place, everything, mine, theirs, norm_gain.reshape(1, 2048), latent_gain.reshape(1, 512),
        cosines, sines, allowed,
    )


def mix(place, everything, attended, mine, theirs, moe_gain):
    def kernel(
        place_ref, in_ref, attended_ref, mine_ref, theirs_ref, gain_ref,
        moe_ref, cols_ref, server_ref, w_first, w_second,
    ):
        c, t = place_ref[3], place_ref[4]

        def visit(j, sources):
            for n, source in enumerate(sources):
                for ref, at in ((mine_ref, c), (theirs_ref, 1 - c)):
                    row = pl.multiple_of(((2 * j + n) * 2 + at) * 16, 16)
                    first, second = ref[source, 0:16, :], ref[source, 16:32, :]
                    w_first[pl.ds(row, 16), :] = first
                    w_second[pl.ds(row, 16), :] = second
                    half = jnp.where(t < 2, first.astype(F32), second.astype(F32))
                    quarter = jnp.where(t % 2 == 0, half[:, 0:256], half[:, 256:512])
                    server_ref[pl.ds(row, 16), :] = quarter.astype(BF)

        in_order(place_ref, visit)
        total = lax.dot_general(
            attended_ref[:, 0:512], w_first[...], NT, preferred_element_type=F32
        ) + lax.dot_general(
            attended_ref[:, 512:1024], w_second[...], NT, preferred_element_type=F32
        )
        mixed = (in_ref[...].astype(F32) + total).astype(BF).astype(F32)
        cols = mixed[:, 0:512]
        for k in range(1, 4):
            cols = jnp.where(t == k, mixed[:, k * 512 : (k + 1) * 512], cols)
        cols_ref[...] = cols.astype(BF)
        moe = rms_norm(mixed, gain_ref[...]).astype(BF)
        moe_ref[0:128, :] = moe[:, 0:1024]
        moe_ref[128:256, :] = moe[:, 1024:2048]

    def whole(*shape):
        return pl.BlockSpec(shape, lambda i: (0,) * len(shape))

    return pl.pallas_call(
        kernel,
        grid=(1,),
        out_shape=[
            jax.ShapeDtypeStruct((256, 1024), BF),
            jax.ShapeDtypeStruct((128, 512), BF),
            jax.ShapeDtypeStruct((2048, 256), BF),
        ],
        in_specs=[SMEM, whole(128, 2048), whole(128, 1024), VMEM, VMEM, whole(1, 2048)],
        out_specs=[whole(256, 1024), whole(128, 512), whole(2048, 256)],
        scratch_shapes=[pltpu.VMEM((2048, 512), BF), pltpu.VMEM((2048, 512), BF)],
        name="mix",
    )(place, everything, attended, mine, theirs, moe_gain.reshape(1, 2048))


def body(
    hidden_in,
    lengths,
    routes,
    gate_weights,
    norm_gain,
    latent_gain,
    moe_gain,
    query_train,
    latent_train,
    expand_train,
    output_train,
    expert_gate,
    expert_up,
    expert_down,
):
    rank = lax.axis_index(T)
    core = lax.axis_index("c")
    place = jnp.stack([lax.axis_index(a) for a in DP + (T,)]).astype(jnp.int32)

    packed = pack_rows(hidden_in, query_train, latent_train, expand_train, output_train)
    everything = lax.all_gather(packed, T, axis=1, tiled=True)
    rows = pick_rows(place, everything)
    gathered = jnp.stack(shifted(rows, "zl"))
    gathered = jnp.stack(shifted(gathered, "y")).reshape(16, 72, 512)
    first_set = gathered[:, :40]
    second_set = gathered[:, 40:]
    first_mine = jnp.stack(ring(first_set, "x")).reshape(64, 40, 512)
    first_theirs = other_core(first_mine)
    second_gated, _ = lax.optimization_barrier((second_set, first_mine))
    second_mine = jnp.stack(ring(second_gated, "x")).reshape(64, 32, 512)
    second_theirs = other_core(second_mine)

    segment, position = positions_of(lengths, TOK)
    segment = segment[0]
    frequency = jnp.exp(jnp.arange(32, dtype=F32) * (-2.0 * math.log(rope_base) / 64))
    angles = position[0].astype(F32)[:, None] * frequency[None, :]
    cosine, sine = jnp.cos(angles), jnp.sin(angles)
    token_index = jnp.arange(TOK, dtype=jnp.int32)
    allowed = (segment[:, None] == segment[None, :]) & (token_index[None, :] <= token_index[:, None])
    attended, latent_normed, key_rope, expand_block = attention(
        place,
        everything,
        first_mine,
        first_theirs,
        norm_gain,
        latent_gain,
        jnp.concatenate([cosine] * 4, axis=1),
        jnp.concatenate([-sine, -sine, sine, sine], axis=1),
        allowed.astype(F32),
    )
    cache_full = jnp.concatenate([latent_normed, key_rope[:, 0:32], key_rope[:, 64:96]], axis=1)
    cache_cols = lax.dynamic_slice_in_dim(cache_full, rank * 144, 144, 1)
    attended_full = lax.all_gather(attended, T, axis=1, tiled=True)
    moe_halves, mixed_cols, output_block = mix(
        place, everything, attended_full, second_mine, second_theirs, moe_gain
    )

    slot_rank = expert_ranks(routes)
    gates = gate_weights.astype(F32)
    pad_ids = jnp.arange(EXPERTS * 2 * PADDED, dtype=jnp.int32)
    pad_core = (pad_ids // PADDED) % 2
    slot_at = routes * (2 * PADDED) + slot_rank
    matches = (pad_ids - pad_core * PADDED)[:, None, None] == slot_at[None, :, :]

    def placed_by(values):
        return jnp.sum(jnp.where(matches, values, 0.0), axis=2)

    placed = placed_by(1.0)
    dispatch = jnp.concatenate(
        [
            jnp.where(pad_core[:, None] == 0, placed, 0.0),
            jnp.where(pad_core[:, None] == 1, placed, 0.0),
        ],
        axis=1,
    ).astype(BF)

    weighted = placed_by(gates[None])
    combine = [jnp.where(pad_core[:, None] == h, weighted, 0.0).astype(BF) for h in range(2)]

    compact = jnp.arange(TOK * CAP, dtype=jnp.int32)
    taken = (compact // CAP) * PADDED + compact % CAP
    squeeze = (jnp.arange(TOK * PADDED, dtype=jnp.int32)[:, None] == taken[None, :]).astype(BF)

    def halves(matrix):
        return (
            lax.dynamic_slice_in_dim(matrix, core * (D // 2), D // 2, 0),
            lax.dynamic_slice_in_dim(matrix, (1 - core) * (D // 2), D // 2, 0),
        )

    gate_mine, gate_other = halves(expert_gate[0])
    up_mine, up_other = halves(expert_up[0])
    around = [(rank + 4 - back) % 4 for back in (0, 1, 3, 2)]
    down_around = jnp.concatenate(
        [lax.dynamic_slice_in_dim(expert_down[0], at * 176, 176, 0) for at in around], axis=0
    )

    def rows_by(weight, rows):
        return lax.dot_general(weight, rows, (((0,), (1,)), ((), ())), preferred_element_type=F32)

    outgoing = jnp.dot(dispatch, moe_halves, preferred_element_type=F32).astype(BF)
    mine = lax.all_to_all(outgoing, DP, split_axis=0, concat_axis=0, tiled=True)
    theirs = other_core(mine)
    gate_part = rows_by(gate_mine, mine) + rows_by(gate_other, theirs)
    up_part = rows_by(up_mine, mine) + rows_by(up_other, theirs)
    hidden = (jax.nn.silu(gate_part) * up_part).astype(BF)

    up_ring = [(j, (j + 1) % 4) for j in range(4)]
    down_ring = [(j, (j + 3) % 4) for j in range(4)]
    own = jnp.dot(hidden, squeeze, preferred_element_type=F32).astype(BF)
    below = lax.ppermute(own, T, up_ring)
    above = lax.ppermute(own, T, down_ring)
    far_first = lax.ppermute(below[:88], T, up_ring)
    far_second = lax.ppermute(above[88:], T, down_ring)

    def out_of(pieces, at):
        rows = jnp.concatenate(pieces, axis=0)
        return lax.dot_general(
            rows, down_around[at : at + rows.shape[0]], (((0,), (0,)), ((), ())),
            preferred_element_type=F32,
        )

    half_out = (out_of([own, below, above], 0) + out_of([far_first, far_second], 528)).astype(BF)
    half_out = jnp.dot(squeeze, half_out, preferred_element_type=F32).astype(BF)
    keep = lax.dynamic_slice_in_dim(half_out, core * 256, 256, 1)
    give = lax.dynamic_slice_in_dim(half_out, (1 - core) * 256, 256, 1)
    both = (keep.astype(F32) + other_core(give).astype(F32)).astype(BF)
    returned = lax.all_to_all(both, DP, split_axis=0, concat_axis=0, tiled=True)
    sums = [
        lax.dot_general(part, returned, (((0,), (0,)), ((), ())), preferred_element_type=F32)
        for part in combine
    ]
    result = mixed_cols.astype(F32)
    hidden_out = (result + jnp.concatenate(sums, axis=1)).astype(BF)
    return (hidden_out, expand_block, output_block, cache_cols)


def solution(mesh):
    fine = Mesh(mesh.devices.reshape(4, 4, 4, 2, 4), DP + (T,))
    rows_both = P(DP + (T,), None)
    in_specs = (
        P(DP, T),
        P(DP, None),
        P(DP, None),
        P(DP, None),
        P(),
        P(),
        P(),
        rows_both,
        rows_both,
        rows_both,
        rows_both,
        P(DP, None, T),
        P(DP, None, T),
        P(DP, None, T),
    )
    out_specs = (P(DP, T), P(None, T), P(None, T), P(DP, T))
    return jax.shard_map(body, mesh=fine, in_specs=in_specs, out_specs=out_specs, check_vma=False)
```

```python
import math

import jax
import jax.numpy as jnp
from jax import lax
from jax.experimental import pallas as pl
from jax.experimental.pallas import tpu as pltpu
from jax.sharding import Mesh
from jax.sharding import PartitionSpec as P

D = 2048
NOPE = 128
ROPE = 64
VDIM = 128
LATENT = 512
EXPERTS = 64
CAP = 14
TOK = 128
LAYER_ROWS = 16 * 4 * CAP

DP = ("zl", "y", "x", "c")
T = "t"
LAYER = ("c", "y", "x")
UP = [(j, (j + 1) % 4) for j in range(4)]
DOWN = [(j, (j + 3) % 4) for j in range(4)]
BF = jnp.bfloat16
F32 = jnp.float32

rope_base = 50000.0


def rms_norm(values, gain_vector):
    mean_square = jnp.mean(values * values, axis=-1, keepdims=True)
    return values * lax.rsqrt(mean_square + 1e-06) * gain_vector


def positions_of(lengths, row_count):
    prompt_ends = jnp.cumsum(lengths, axis=1)
    starts = prompt_ends - lengths
    token_index = jnp.arange(row_count, dtype=jnp.int32)
    segment = jnp.sum(
        (token_index[None, :, None] >= prompt_ends[:, None, :]).astype(jnp.int32), axis=2
    )
    member = segment[:, :, None] == jnp.arange(lengths.shape[1], dtype=jnp.int32)[None, None, :]
    offset = jnp.sum(jnp.where(member, starts[:, None, :], 0), axis=2)
    return (segment, token_index[None, :] - offset)


def expert_ranks(routes):
    experts = jnp.arange(EXPERTS, dtype=jnp.int32)[None, :, None]
    named = [(routes[:, k : k + 1] == experts) for k in range(6)]
    per_token = sum(n.astype(F32) for n in named).astype(BF)
    index = jnp.arange(TOK, dtype=jnp.int32)
    earlier = (index[:, None] < index[None, :]).astype(BF)
    before = lax.dot_general(
        per_token, earlier, (((2,), (0,)), ((), ())), preferred_element_type=F32
    )
    ranks = [jnp.sum(jnp.where(n, before, 0.0), axis=1) for n in named]
    return jnp.stack(ranks, axis=1).astype(jnp.int32)


def shifted(block, axis):
    return [block] + [
        lax.ppermute(block, axis, [(j, (j + s) % 4) for j in range(4)]) for s in range(1, 4)
    ]


def ring(block, axis):
    half = block.shape[0] // 2
    below, above = lax.ppermute(block, axis, UP), lax.ppermute(block, axis, DOWN)
    far = [lax.ppermute(below[:half], axis, UP), lax.ppermute(above[half:], axis, DOWN)]
    return [block, below, jnp.concatenate(far), above]


def other_core(block):
    return lax.ppermute(block, "c", [(0, 1), (1, 0)])


VMEM = pl.BlockSpec(memory_space=pltpu.VMEM)
SMEM = pl.BlockSpec(memory_space=pltpu.SMEM)
NT = (((1,), (1,)), ((), ()))


def pack_rows(hidden_in, query, latent, expand, output):
    def kernel(hidden_ref, q_ref, l_ref, e_ref, o_ref, out_ref, rows):
        out_ref[0:128, :] = hidden_ref[...]
        tail_a, tail_b = l_ref[:, 512:544], l_ref[:, 544:576]
        tail = [tail_a, tail_a, tail_b, tail_b]
        for t in range(4):
            q = q_ref[:, t * 384 : (t + 1) * 384]
            parts = [
                q[:, 0:128], q[:, 192:320],
                q[:, 128:160], q[:, 320:352], q[:, 160:192], q[:, 352:384],
            ]
            rows[t * 4 : t * 4 + 4, :] = jnp.concatenate(parts + tail, axis=1)
            rows[20 + t : 21 + t, :] = e_ref[:, t * 512 : (t + 1) * 512]
        rows[16:20, :] = l_ref[:, 0:512]
        rows[24:28, :] = o_ref[:, 0:512]
        rows[28:32, :] = o_ref[:, 512:1024]
        out_ref[128:160, :] = rows[...].astype(BF)

    return pl.pallas_call(
        kernel,
        out_shape=jax.ShapeDtypeStruct((160, 512), BF),
        in_specs=[VMEM] * 5,
        out_specs=VMEM,
        scratch_shapes=[pltpu.VMEM((32, 512), F32)],
        name="pack_rows",
    )(hidden_in, query, latent, expand, output)


def pick_rows(place, everything, routes, gates):
    def kernel(place_ref, in_ref, routes_ref, gates_ref, out_ref, wide, rows):
        t = place_ref[4]
        wide[...] = in_ref[...].astype(F32)
        for s in range(4):
            lanes = slice(s * 512, (s + 1) * 512)
            q = wide[0:4, lanes]
            e = wide[20:21, lanes]
            for k in range(1, 4):
                q = jnp.where(t == k, wide[k * 4 : k * 4 + 4, lanes], q)
                e = jnp.where(t == k, wide[20 + k : 21 + k, lanes], e)
            rows[s * 4 : s * 4 + 4, :] = q
            rows[16 + s * 4 : 20 + s * 4, :] = wide[16:20, lanes]
            rows[32 + s : 33 + s, :] = e
            rows[36 + s : 37 + s, :] = e
            rows[40 + s * 4 : 44 + s * 4, :] = wide[24:28, lanes]
            rows[56 + s * 4 : 60 + s * 4, :] = wide[28:32, lanes]
        rows[72:88, :] = jnp.zeros((16, 512), F32)
        rows[72:78, 0:128] = routes_ref[...].astype(F32)
        rows[80:86, 0:128] = gates_ref[...].astype(F32)
        out_ref[...] = rows[...].astype(BF)

    def small(rows):
        return pl.BlockSpec((rows, 128), lambda i: (0, 0))

    return pl.pallas_call(
        kernel,
        grid=(1,),
        out_shape=jax.ShapeDtypeStruct((88, 512), BF),
        in_specs=[SMEM, pl.BlockSpec((32, 2048), lambda i: (4, 0)), small(6), small(6)],
        out_specs=pl.BlockSpec((88, 512), lambda i: (0, 0)),
        scratch_shapes=[pltpu.VMEM((32, 2048), F32), pltpu.VMEM((88, 512), F32)],
        name="pick_rows",
    )(place, everything, routes.T, gates.T)


def in_order(place_ref, visit):
    zl, y, x = place_ref[0], place_ref[1], place_ref[2]

    def source_of(i):
        row_zl, row_y, row_x = i // 16, (i // 4) % 4, i % 4
        return ((x - row_x + 4) % 4 * 4 + (y - row_y + 4) % 4) * 4 + (zl - row_zl + 4) % 4

    def step(j, carry):
        visit(j, (source_of(2 * j), source_of(2 * j + 1)))
        return carry

    lax.fori_loop(0, 32, step, 0)


def attention(place, everything, mine, theirs, norm_gain, latent_gain, cosines, sines, allowed):
    def kernel(
        place_ref, in_ref, mine_ref, theirs_ref, norm_ref, gain_ref, cos_ref, sin_ref, allowed_ref,
        attended_ref, latent_ref, rope_ref, expand_ref, q_rows, l_rows,
    ):
        c = place_ref[3]
        low = lax.broadcasted_iota(jnp.int32, (8, 512), 0) < 4

        def visit(j, sources):
            pair = []
            for n, source in enumerate(sources):
                for ref, at in ((mine_ref, c), (theirs_ref, 1 - c)):
                    row = pl.multiple_of(((2 * j + n) * 2 + at) * 16, 16)
                    q_rows[pl.ds(row, 16), :] = ref[source, 0:16, :]
                    l_rows[pl.ds(row, 16), :] = ref[source, 16:32, :]
                own = mine_ref[source, 32:40, :].astype(F32)
                other = theirs_ref[source, 32:40, :].astype(F32)
                first = jnp.where(c == 0, own, other)
                second = jnp.where(c == 0, other, own)
                pair.append(jnp.where(low, first, second))
            row = pl.multiple_of(j * 16, 16)
            expand_ref[pl.ds(row, 16), :] = jnp.concatenate(pair, axis=0).astype(BF)

        in_order(place_ref, visit)
        normed = rms_norm(in_ref[...].astype(F32), norm_ref[...]).astype(BF)
        query = jnp.dot(normed, q_rows[...], preferred_element_type=F32)
        latent = jnp.dot(normed, l_rows[...], preferred_element_type=F32).astype(BF)
        latent = rms_norm(latent.astype(F32), gain_ref[...]).astype(BF)
        latent_ref[...] = latent
        cosine, sine = cos_ref[...], sin_ref[...]

        def rotated(v):
            return (v * cosine + pltpu.roll(v, 64, 1) * sine).astype(BF)

        key_rope = rotated(query[:, 384:512].astype(BF).astype(F32))
        rope_ref[...] = key_rope
        query_rope = rotated(query[:, 256:384])
        expanded = jnp.dot(latent, expand_ref[...], preferred_element_type=F32).astype(BF)
        head_of = (lax.broadcasted_iota(jnp.int32, (128, 128), 1) // 32) % 2
        for h in range(2):
            own_rope = jnp.where(head_of == h, query_rope.astype(F32), 0.0).astype(BF)
            scores = lax.dot_general(
                query[:, h * 128 : (h + 1) * 128].astype(BF),
                expanded[:, h * 256 : h * 256 + 128],
                NT,
                preferred_element_type=F32,
            )
            scores = scores + lax.dot_general(own_rope, key_rope, NT, preferred_element_type=F32)
            scores = scores * (1.0 / math.sqrt(NOPE + ROPE))
            scores = jnp.where(allowed_ref[...] > 0.0, scores, -1e30)
            powers = jnp.exp(scores - jnp.max(scores, axis=-1, keepdims=True))
            probs = (powers / jnp.sum(powers, axis=-1, keepdims=True)).astype(BF)
            out = jnp.dot(
                probs, expanded[:, h * 256 + 128 : h * 256 + 256], preferred_element_type=F32
            )
            attended_ref[:, h * 128 : (h + 1) * 128] = out.astype(BF)

    def whole(*shape):
        return pl.BlockSpec(shape, lambda i: (0,) * len(shape))

    return pl.pallas_call(
        kernel,
        grid=(1,),
        out_shape=[
            jax.ShapeDtypeStruct((128, 256), BF),
            jax.ShapeDtypeStruct((128, 512), BF),
            jax.ShapeDtypeStruct((128, 128), BF),
            jax.ShapeDtypeStruct((512, 512), BF),
        ],
        in_specs=[
            SMEM, whole(128, 2048), VMEM, VMEM,
            whole(1, 2048), whole(1, 512), whole(128, 128), whole(128, 128), whole(128, 128),
        ],
        out_specs=[whole(128, 256), whole(128, 512), whole(128, 128), whole(512, 512)],
        scratch_shapes=[pltpu.VMEM((2048, 512), BF), pltpu.VMEM((2048, 512), BF)],
        name="attention",
    )(
        place, everything, mine, theirs, norm_gain.reshape(1, 2048), latent_gain.reshape(1, 512),
        cosines, sines, allowed,
    )


def mix(place, everything, attended, mine, theirs, moe_gain):
    def kernel(
        place_ref, in_ref, attended_ref, mine_ref, theirs_ref, gain_ref,
        moe_ref, cols_ref, server_ref, w_first, w_second,
    ):
        c, t = place_ref[3], place_ref[4]

        def visit(j, sources):
            for n, source in enumerate(sources):
                for ref, at in ((mine_ref, c), (theirs_ref, 1 - c)):
                    row = pl.multiple_of(((2 * j + n) * 2 + at) * 16, 16)
                    first, second = ref[source, 0:16, :], ref[source, 16:32, :]
                    w_first[pl.ds(row, 16), :] = first
                    w_second[pl.ds(row, 16), :] = second
                    half = jnp.where(t < 2, first.astype(F32), second.astype(F32))
                    quarter = jnp.where(t % 2 == 0, half[:, 0:256], half[:, 256:512])
                    server_ref[pl.ds(row, 16), :] = quarter.astype(BF)

        in_order(place_ref, visit)
        total = lax.dot_general(
            attended_ref[:, 0:512], w_first[...], NT, preferred_element_type=F32
        ) + lax.dot_general(
            attended_ref[:, 512:1024], w_second[...], NT, preferred_element_type=F32
        )
        mixed = (in_ref[...].astype(F32) + total).astype(BF).astype(F32)
        cols = mixed[:, 0:512]
        for k in range(1, 4):
            cols = jnp.where(t == k, mixed[:, k * 512 : (k + 1) * 512], cols)
        cols_ref[...] = cols.astype(BF)
        moe = rms_norm(mixed, gain_ref[...]).astype(BF)
        moe_ref[0:128, :] = moe[:, 0:1024]
        moe_ref[128:256, :] = moe[:, 1024:2048]

    def whole(*shape):
        return pl.BlockSpec(shape, lambda i: (0,) * len(shape))

    return pl.pallas_call(
        kernel,
        grid=(1,),
        out_shape=[
            jax.ShapeDtypeStruct((256, 1024), BF),
            jax.ShapeDtypeStruct((128, 512), BF),
            jax.ShapeDtypeStruct((2048, 256), BF),
        ],
        in_specs=[SMEM, whole(128, 2048), whole(128, 1024), VMEM, VMEM, whole(1, 2048)],
        out_specs=[whole(256, 1024), whole(128, 512), whole(2048, 256)],
        scratch_shapes=[pltpu.VMEM((2048, 512), BF), pltpu.VMEM((2048, 512), BF)],
        name="mix",
    )(place, everything, attended, mine, theirs, moe_gain.reshape(1, 2048))


def body(
    hidden_in,
    lengths,
    routes,
    gate_weights,
    norm_gain,
    latent_gain,
    moe_gain,
    query_train,
    latent_train,
    expand_train,
    output_train,
    expert_gate,
    expert_up,
    expert_down,
):
    rank = lax.axis_index(T)
    core = lax.axis_index("c")
    place = jnp.stack([lax.axis_index(a) for a in DP + (T,)]).astype(jnp.int32)

    packed = pack_rows(hidden_in, query_train, latent_train, expand_train, output_train)
    everything = lax.all_gather(packed, T, axis=1, tiled=True)
    rows = pick_rows(place, everything, routes, gate_weights)
    gathered = jnp.stack(shifted(rows, "zl"))
    column_routes = gathered[:, 72:78, 0:128].astype(jnp.int32)
    column_gates = gathered[:, 80:86, 0:128].astype(F32)
    gathered = jnp.stack(shifted(gathered[:, :72], "y")).reshape(16, 72, 512)
    first_set = gathered[:, :40]
    first_mine = jnp.stack(ring(first_set, "x")).reshape(64, 40, 512)
    first_theirs = other_core(first_mine)
    second_set, _ = lax.optimization_barrier((gathered[:, 40:], first_mine))
    second_below = lax.ppermute(second_set, "x", UP)
    second_above = lax.ppermute(second_set, "x", DOWN)

    segment, position = positions_of(lengths, TOK)
    segment = segment[0]
    frequency = jnp.exp(jnp.arange(32, dtype=F32) * (-2.0 * math.log(rope_base) / 64))
    angles = position[0].astype(F32)[:, None] * frequency[None, :]
    cosine, sine = jnp.cos(angles), jnp.sin(angles)
    token_index = jnp.arange(TOK, dtype=jnp.int32)
    allowed = (segment[:, None] == segment[None, :]) & (token_index[None, :] <= token_index[:, None])
    attended, latent_normed, key_rope, expand_block = attention(
        place,
        everything,
        first_mine,
        first_theirs,
        norm_gain,
        latent_gain,
        jnp.concatenate([cosine] * 4, axis=1),
        jnp.concatenate([-sine, -sine, sine, sine], axis=1),
        allowed.astype(F32),
    )
    cache_full = jnp.concatenate([latent_normed, key_rope[:, 0:32], key_rope[:, 64:96]], axis=1)
    cache_cols = lax.dynamic_slice_in_dim(cache_full, rank * 144, 144, 1)
    below_part, above_part, attended = lax.optimization_barrier(
        (second_below[:8], second_above[8:], attended)
    )
    second_far = jnp.concatenate(
        [lax.ppermute(below_part, "x", UP), lax.ppermute(above_part, "x", DOWN)]
    )
    attended_full = lax.all_gather(attended, T, axis=1, tiled=True)
    second_mine = jnp.stack([second_set, second_below, second_far, second_above]).reshape(64, 32, 512)
    second_theirs = other_core(second_mine)
    moe_halves, mixed_cols, output_block = mix(
        place, everything, attended_full, second_mine, second_theirs, moe_gain
    )

    slot_rank = expert_ranks(column_routes)
    local = column_routes - lax.axis_index("zl") * 16
    group = jnp.arange(4, dtype=jnp.int32)[:, None, None]
    target = jnp.where(
        (local >= 0) & (local < 16), local * (4 * CAP) + group * CAP + slot_rank, -1
    )
    row_ids = jnp.arange(LAYER_ROWS, dtype=jnp.int32)[:, None]
    dispatch = jnp.zeros((LAYER_ROWS, 4 * TOK), F32)
    combine = jnp.zeros((LAYER_ROWS, 4 * TOK), F32)
    for k in range(6):
        hit = row_ids == target[:, k].reshape(1, 4 * TOK)
        dispatch = dispatch + hit.astype(F32)
        combine = combine + jnp.where(hit, column_gates[:, k].reshape(1, 4 * TOK), 0.0)
    dispatch = jnp.broadcast_to(dispatch.astype(BF)[None], (2, LAYER_ROWS, 4 * TOK))
    combine = jnp.broadcast_to(combine.astype(BF)[None], (2, LAYER_ROWS, 4 * TOK))

    def halves(matrix):
        return (
            lax.dynamic_slice_in_dim(matrix, core * (D // 2), D // 2, 0),
            lax.dynamic_slice_in_dim(matrix, (1 - core) * (D // 2), D // 2, 0),
        )

    gate_mine, gate_other = halves(expert_gate[0])
    up_mine, up_other = halves(expert_up[0])
    around = [(rank + 4 - back) % 4 for back in (0, 1, 3, 2)]
    down_around = jnp.concatenate(
        [lax.dynamic_slice_in_dim(expert_down[0], at * 176, 176, 0) for at in around], axis=0
    )

    def rows_by(weight, rows):
        return lax.dot_general(weight, rows, (((0,), (1,)), ((), ())), preferred_element_type=F32)

    at_z = [(z % 4) * 4 + z // 4 for z in range(16)]
    z_up = [(at_z[z], at_z[(z + 1) % 16]) for z in range(16)]
    z_down = [(at_z[z], at_z[(z + 15) % 16]) for z in range(16)]
    back_one = lax.ppermute(moe_halves, ("zl", T), z_up)
    on_one = lax.ppermute(moe_halves, ("zl", T), z_down)
    far_left = lax.ppermute(back_one[:TOK], ("zl", T), z_up)
    far_right = lax.ppermute(on_one[TOK:], ("zl", T), z_down)
    tokens = jnp.stack(
        [
            jnp.concatenate([moe_halves[:TOK], back_one[:TOK], far_left, on_one[:TOK]]),
            jnp.concatenate([moe_halves[TOK:], back_one[TOK:], far_right, on_one[TOK:]]),
        ]
    )
    outgoing = lax.dot_general(
        dispatch, tokens, (((2,), (1,)), ((0,), (0,))), preferred_element_type=F32
    ).astype(BF)
    mine = lax.all_to_all(
        outgoing.reshape(2 * LAYER_ROWS, D // 2), LAYER, split_axis=0, concat_axis=0, tiled=True
    )
    theirs = other_core(mine)
    gate_part = rows_by(gate_mine, mine) + rows_by(gate_other, theirs)
    up_part = rows_by(up_mine, mine) + rows_by(up_other, theirs)
    own = (jax.nn.silu(gate_part) * up_part).astype(BF)

    below = lax.ppermute(own, T, UP)
    above = lax.ppermute(own, T, DOWN)
    far_first = lax.ppermute(below[:88], T, UP)
    far_second = lax.ppermute(above[88:], T, DOWN)

    def out_of(pieces, at):
        rows = jnp.concatenate(pieces, axis=0)
        return lax.dot_general(
            rows, down_around[at : at + rows.shape[0]], (((0,), (0,)), ((), ())),
            preferred_element_type=F32,
        )

    half_out = (out_of([own, below, above], 0) + out_of([far_first, far_second], 528)).astype(BF)
    keep = lax.dynamic_slice_in_dim(half_out, core * 256, 256, 1)
    give = lax.dynamic_slice_in_dim(half_out, (1 - core) * 256, 256, 1)
    both = (keep.astype(F32) + other_core(give).astype(F32)).astype(BF)
    returned = lax.all_to_all(both, LAYER, split_axis=0, concat_axis=0, tiled=True)
    partial = lax.dot_general(
        combine,
        returned.reshape(2, LAYER_ROWS, 256),
        (((1,), (1,)), ((0,), (0,))),
        preferred_element_type=F32,
    ).reshape(2, 4, TOK, 256)
    sums = partial[:, 0]
    for s in range(1, 4):
        sent = partial[:, s].astype(BF)
        sums = sums + lax.ppermute(sent, "zl", [(j, (j - s) % 4) for j in range(4)]).astype(F32)
    result = mixed_cols.astype(F32)
    hidden_out = (result + jnp.concatenate([sums[0], sums[1]], axis=1)).astype(BF)
    return (hidden_out, expand_block, output_block, cache_cols)


def solution(mesh):
    fine = Mesh(mesh.devices.reshape(4, 4, 4, 2, 4), DP + (T,))
    rows_both = P(DP + (T,), None)
    in_specs = (
        P(DP, T),
        P(DP, None),
        P(DP, None),
        P(DP, None),
        P(),
        P(),
        P(),
        rows_both,
        rows_both,
        rows_both,
        rows_both,
        P(DP, None, T),
        P(DP, None, T),
        P(DP, None, T),
    )
    out_specs = (P(DP, T), P(None, T), P(None, T), P(DP, T))
    return jax.shard_map(body, mesh=fine, in_specs=in_specs, out_specs=out_specs, check_vma=False)
```

```python
import math

import jax
import jax.numpy as jnp
from jax import lax
from jax.experimental import pallas as pl
from jax.experimental.pallas import tpu as pltpu
from jax.sharding import Mesh
from jax.sharding import PartitionSpec as P

D = 2048
NOPE = 128
ROPE = 64
VDIM = 128
LATENT = 512
EXPERTS = 64
CAP = 14
TOK = 128
LAYER_ROWS = 16 * 4 * CAP

DP = ("zl", "y", "x", "c")
T = "t"
LAYER = ("c", "y", "x")
UP = [(j, (j + 1) % 4) for j in range(4)]
DOWN = [(j, (j + 3) % 4) for j in range(4)]
BF = jnp.bfloat16
F32 = jnp.float32

rope_base = 50000.0


def rms_norm(values, gain_vector):
    mean_square = jnp.mean(values * values, axis=-1, keepdims=True)
    return values * lax.rsqrt(mean_square + 1e-06) * gain_vector


def positions_of(lengths, row_count):
    prompt_ends = jnp.cumsum(lengths, axis=1)
    starts = prompt_ends - lengths
    token_index = jnp.arange(row_count, dtype=jnp.int32)
    segment = jnp.sum(
        (token_index[None, :, None] >= prompt_ends[:, None, :]).astype(jnp.int32), axis=2
    )
    member = segment[:, :, None] == jnp.arange(lengths.shape[1], dtype=jnp.int32)[None, None, :]
    offset = jnp.sum(jnp.where(member, starts[:, None, :], 0), axis=2)
    return (segment, token_index[None, :] - offset)


def expert_ranks(routes):
    experts = jnp.arange(EXPERTS, dtype=jnp.int32)[None, :, None]
    named = [(routes[:, k : k + 1] == experts) for k in range(6)]
    per_token = sum(n.astype(F32) for n in named).astype(BF)
    index = jnp.arange(TOK, dtype=jnp.int32)
    earlier = (index[:, None] < index[None, :]).astype(BF)
    before = lax.dot_general(
        per_token, earlier, (((2,), (0,)), ((), ())), preferred_element_type=F32
    )
    ranks = [jnp.sum(jnp.where(n, before, 0.0), axis=1) for n in named]
    return jnp.stack(ranks, axis=1).astype(jnp.int32)


def shifted(block, axis):
    return [block] + [
        lax.ppermute(block, axis, [(j, (j + s) % 4) for j in range(4)]) for s in range(1, 4)
    ]


def ring(block, axis):
    half = block.shape[0] // 2
    below, above = lax.ppermute(block, axis, UP), lax.ppermute(block, axis, DOWN)
    far = [lax.ppermute(below[:half], axis, UP), lax.ppermute(above[half:], axis, DOWN)]
    return [block, below, jnp.concatenate(far), above]


def other_core(block):
    return lax.ppermute(block, "c", [(0, 1), (1, 0)])


VMEM = pl.BlockSpec(memory_space=pltpu.VMEM)
SMEM = pl.BlockSpec(memory_space=pltpu.SMEM)
NT = (((1,), (1,)), ((), ()))


def pack_rows(hidden_in, query, latent, expand, output):
    def kernel(hidden_ref, q_ref, l_ref, e_ref, o_ref, out_ref, rows):
        out_ref[0:128, :] = hidden_ref[...]
        tail_a, tail_b = l_ref[:, 512:544], l_ref[:, 544:576]
        tail = [tail_a, tail_a, tail_b, tail_b]
        for t in range(4):
            q = q_ref[:, t * 384 : (t + 1) * 384]
            parts = [
                q[:, 0:128], q[:, 192:320],
                q[:, 128:160], q[:, 320:352], q[:, 160:192], q[:, 352:384],
            ]
            rows[t * 4 : t * 4 + 4, :] = jnp.concatenate(parts + tail, axis=1)
            rows[20 + t : 21 + t, :] = e_ref[:, t * 512 : (t + 1) * 512]
        rows[16:20, :] = l_ref[:, 0:512]
        rows[24:28, :] = o_ref[:, 0:512]
        rows[28:32, :] = o_ref[:, 512:1024]
        out_ref[128:160, :] = rows[...].astype(BF)

    return pl.pallas_call(
        kernel,
        out_shape=jax.ShapeDtypeStruct((160, 512), BF),
        in_specs=[VMEM] * 5,
        out_specs=VMEM,
        scratch_shapes=[pltpu.VMEM((32, 512), F32)],
        name="pack_rows",
    )(hidden_in, query, latent, expand, output)


def pick_rows(place, everything, routes, gates):
    def kernel(place_ref, in_ref, routes_ref, gates_ref, out_ref, wide, rows):
        t = place_ref[4]
        wide[...] = in_ref[...].astype(F32)
        for s in range(4):
            lanes = slice(s * 512, (s + 1) * 512)
            q = wide[0:4, lanes]
            e = wide[20:21, lanes]
            for k in range(1, 4):
                q = jnp.where(t == k, wide[k * 4 : k * 4 + 4, lanes], q)
                e = jnp.where(t == k, wide[20 + k : 21 + k, lanes], e)
            rows[s * 4 : s * 4 + 4, :] = q
            rows[16 + s * 4 : 20 + s * 4, :] = wide[16:20, lanes]
            rows[32 + s : 33 + s, :] = e
            rows[36 + s : 37 + s, :] = e
            rows[40 + s * 4 : 44 + s * 4, :] = wide[24:28, lanes]
            rows[56 + s * 4 : 60 + s * 4, :] = wide[28:32, lanes]
        rows[72:88, :] = jnp.zeros((16, 512), F32)
        rows[72:78, 0:128] = routes_ref[...].astype(F32)
        rows[80:86, 0:128] = gates_ref[...].astype(F32)
        out_ref[...] = rows[...].astype(BF)

    def small(rows):
        return pl.BlockSpec((rows, 128), lambda i: (0, 0))

    return pl.pallas_call(
        kernel,
        grid=(1,),
        out_shape=jax.ShapeDtypeStruct((88, 512), BF),
        in_specs=[SMEM, pl.BlockSpec((32, 2048), lambda i: (4, 0)), small(6), small(6)],
        out_specs=pl.BlockSpec((88, 512), lambda i: (0, 0)),
        scratch_shapes=[pltpu.VMEM((32, 2048), F32), pltpu.VMEM((88, 512), F32)],
        name="pick_rows",
    )(place, everything, routes.T, gates.T)


def in_order(place_ref, visit):
    zl, y, x = place_ref[0], place_ref[1], place_ref[2]

    def source_of(i):
        row_zl, row_y, row_x = i // 16, (i // 4) % 4, i % 4
        return ((x - row_x + 4) % 4 * 4 + (y - row_y + 4) % 4) * 4 + (zl - row_zl + 4) % 4

    def step(j, carry):
        visit(j, (source_of(2 * j), source_of(2 * j + 1)))
        return carry

    lax.fori_loop(0, 32, step, 0)


def attention(place, everything, mine, theirs, norm_gain, latent_gain, cosines, sines, allowed):
    def kernel(
        place_ref, in_ref, mine_ref, theirs_ref, norm_ref, gain_ref, cos_ref, sin_ref, allowed_ref,
        attended_ref, latent_ref, rope_ref, expand_ref, q_rows, l_rows,
    ):
        c = place_ref[3]
        low = lax.broadcasted_iota(jnp.int32, (8, 512), 0) < 4

        def visit(j, sources):
            pair = []
            for n, source in enumerate(sources):
                for ref, at in ((mine_ref, c), (theirs_ref, 1 - c)):
                    row = pl.multiple_of(((2 * j + n) * 2 + at) * 16, 16)
                    q_rows[pl.ds(row, 16), :] = ref[source, 0:16, :]
                    l_rows[pl.ds(row, 16), :] = ref[source, 16:32, :]
                own = mine_ref[source, 32:40, :].astype(F32)
                other = theirs_ref[source, 32:40, :].astype(F32)
                first = jnp.where(c == 0, own, other)
                second = jnp.where(c == 0, other, own)
                pair.append(jnp.where(low, first, second))
            row = pl.multiple_of(j * 16, 16)
            expand_ref[pl.ds(row, 16), :] = jnp.concatenate(pair, axis=0).astype(BF)

        in_order(place_ref, visit)
        normed = rms_norm(in_ref[...].astype(F32), norm_ref[...]).astype(BF)
        query = jnp.dot(normed, q_rows[...], preferred_element_type=F32)
        latent = jnp.dot(normed, l_rows[...], preferred_element_type=F32).astype(BF)
        latent = rms_norm(latent.astype(F32), gain_ref[...]).astype(BF)
        latent_ref[...] = latent
        cosine, sine = cos_ref[...], sin_ref[...]

        def rotated(v):
            return (v * cosine + pltpu.roll(v, 64, 1) * sine).astype(BF)

        key_rope = rotated(query[:, 384:512].astype(BF).astype(F32))
        rope_ref[...] = key_rope
        query_rope = rotated(query[:, 256:384])
        expanded = jnp.dot(latent, expand_ref[...], preferred_element_type=F32).astype(BF)
        head_of = (lax.broadcasted_iota(jnp.int32, (128, 128), 1) // 32) % 2
        for h in range(2):
            own_rope = jnp.where(head_of == h, query_rope.astype(F32), 0.0).astype(BF)
            scores = lax.dot_general(
                query[:, h * 128 : (h + 1) * 128].astype(BF),
                expanded[:, h * 256 : h * 256 + 128],
                NT,
                preferred_element_type=F32,
            )
            scores = scores + lax.dot_general(own_rope, key_rope, NT, preferred_element_type=F32)
            scores = scores * (1.0 / math.sqrt(NOPE + ROPE))
            scores = jnp.where(allowed_ref[...] > 0.0, scores, -1e30)
            powers = jnp.exp(scores - jnp.max(scores, axis=-1, keepdims=True))
            probs = (powers / jnp.sum(powers, axis=-1, keepdims=True)).astype(BF)
            out = jnp.dot(
                probs, expanded[:, h * 256 + 128 : h * 256 + 256], preferred_element_type=F32
            )
            attended_ref[:, h * 128 : (h + 1) * 128] = out.astype(BF)

    def whole(*shape):
        return pl.BlockSpec(shape, lambda i: (0,) * len(shape))

    return pl.pallas_call(
        kernel,
        grid=(1,),
        out_shape=[
            jax.ShapeDtypeStruct((128, 256), BF),
            jax.ShapeDtypeStruct((128, 512), BF),
            jax.ShapeDtypeStruct((128, 128), BF),
            jax.ShapeDtypeStruct((512, 512), BF),
        ],
        in_specs=[
            SMEM, whole(128, 2048), VMEM, VMEM,
            whole(1, 2048), whole(1, 512), whole(128, 128), whole(128, 128), whole(128, 128),
        ],
        out_specs=[whole(128, 256), whole(128, 512), whole(128, 128), whole(512, 512)],
        scratch_shapes=[pltpu.VMEM((2048, 512), BF), pltpu.VMEM((2048, 512), BF)],
        name="attention",
    )(
        place, everything, mine, theirs, norm_gain.reshape(1, 2048), latent_gain.reshape(1, 512),
        cosines, sines, allowed,
    )


def mix(place, everything, attended, mine, theirs, moe_gain):
    def kernel(
        place_ref, in_ref, attended_ref, mine_ref, theirs_ref, gain_ref,
        moe_ref, left_ref, right_ref, cols_ref, server_ref, w_first, w_second,
    ):
        c, t = place_ref[3], place_ref[4]

        def visit(j, sources):
            for n, source in enumerate(sources):
                for ref, at in ((mine_ref, c), (theirs_ref, 1 - c)):
                    row = pl.multiple_of(((2 * j + n) * 2 + at) * 16, 16)
                    first, second = ref[source, 0:16, :], ref[source, 16:32, :]
                    w_first[pl.ds(row, 16), :] = first
                    w_second[pl.ds(row, 16), :] = second
                    half = jnp.where(t < 2, first.astype(F32), second.astype(F32))
                    quarter = jnp.where(t % 2 == 0, half[:, 0:256], half[:, 256:512])
                    server_ref[pl.ds(row, 16), :] = quarter.astype(BF)

        in_order(place_ref, visit)
        total = lax.dot_general(
            attended_ref[:, 0:512], w_first[...], NT, preferred_element_type=F32
        ) + lax.dot_general(
            attended_ref[:, 512:1024], w_second[...], NT, preferred_element_type=F32
        )
        mixed = (in_ref[...].astype(F32) + total).astype(BF).astype(F32)
        cols = mixed[:, 0:512]
        for k in range(1, 4):
            cols = jnp.where(t == k, mixed[:, k * 512 : (k + 1) * 512], cols)
        cols_ref[...] = cols.astype(BF)
        moe = rms_norm(mixed, gain_ref[...]).astype(BF)
        moe_ref[0:128, :] = moe[:, 0:1024]
        moe_ref[128:256, :] = moe[:, 1024:2048]
        left_ref[...] = moe[:, 0:1024]
        right_ref[...] = moe[:, 1024:2048]

    def whole(*shape):
        return pl.BlockSpec(shape, lambda i: (0,) * len(shape))

    return pl.pallas_call(
        kernel,
        grid=(1,),
        out_shape=[
            jax.ShapeDtypeStruct((256, 1024), BF),
            jax.ShapeDtypeStruct((128, 1024), BF),
            jax.ShapeDtypeStruct((128, 1024), BF),
            jax.ShapeDtypeStruct((128, 512), BF),
            jax.ShapeDtypeStruct((2048, 256), BF),
        ],
        in_specs=[SMEM, whole(128, 2048), whole(128, 1024), VMEM, VMEM, whole(1, 2048)],
        out_specs=[
            whole(256, 1024), whole(128, 1024), whole(128, 1024), whole(128, 512), whole(2048, 256)
        ],
        scratch_shapes=[pltpu.VMEM((2048, 512), BF), pltpu.VMEM((2048, 512), BF)],
        name="mix",
    )(place, everything, attended, mine, theirs, moe_gain.reshape(1, 2048))


def body(
    hidden_in,
    lengths,
    routes,
    gate_weights,
    norm_gain,
    latent_gain,
    moe_gain,
    query_train,
    latent_train,
    expand_train,
    output_train,
    expert_gate,
    expert_up,
    expert_down,
):
    rank = lax.axis_index(T)
    core = lax.axis_index("c")
    place = jnp.stack([lax.axis_index(a) for a in DP + (T,)]).astype(jnp.int32)

    packed = pack_rows(hidden_in, query_train, latent_train, expand_train, output_train)
    everything = lax.all_gather(packed, T, axis=1, tiled=True)
    rows = pick_rows(place, everything, routes, gate_weights)
    gathered = jnp.stack(shifted(rows, "zl"))
    column_routes = gathered[:, 72:78, 0:128].astype(jnp.int32)
    column_gates = gathered[:, 80:86, 0:128].astype(F32)
    down_mine, _ = lax.optimization_barrier((expert_down[0], column_routes))
    below_a = lax.ppermute(down_mine[:352], T, UP)
    above_a = lax.ppermute(down_mine[352:], T, DOWN)
    gathered = jnp.stack(shifted(gathered[:, :72], "y")).reshape(16, 72, 512)
    first_set = gathered[:, :40]
    first_mine = jnp.stack(ring(first_set, "x")).reshape(64, 40, 512)
    first_mine, below_a, above_a, down_mine = lax.optimization_barrier(
        (first_mine, below_a, above_a, down_mine)
    )
    first_theirs = other_core(first_mine)
    below_b = lax.ppermute(down_mine[352:], T, UP)
    above_b = lax.ppermute(down_mine[:352], T, DOWN)
    second_set, _ = lax.optimization_barrier((gathered[:, 40:], first_theirs))
    second_below = lax.ppermute(second_set, "x", UP)
    second_above = lax.ppermute(second_set, "x", DOWN)

    segment, position = positions_of(lengths, TOK)
    segment = segment[0]
    frequency = jnp.exp(jnp.arange(32, dtype=F32) * (-2.0 * math.log(rope_base) / 64))
    angles = position[0].astype(F32)[:, None] * frequency[None, :]
    cosine, sine = jnp.cos(angles), jnp.sin(angles)
    token_index = jnp.arange(TOK, dtype=jnp.int32)
    allowed = (segment[:, None] == segment[None, :]) & (token_index[None, :] <= token_index[:, None])
    attended, latent_normed, key_rope, expand_block = attention(
        place,
        everything,
        first_mine,
        first_theirs,
        norm_gain,
        latent_gain,
        jnp.concatenate([cosine] * 4, axis=1),
        jnp.concatenate([-sine, -sine, sine, sine], axis=1),
        allowed.astype(F32),
    )
    cache_full = jnp.concatenate([latent_normed, key_rope[:, 0:32], key_rope[:, 64:96]], axis=1)
    cache_cols = lax.dynamic_slice_in_dim(cache_full, rank * 144, 144, 1)
    second_below, second_above, attended = lax.optimization_barrier(
        (second_below, second_above, attended)
    )
    far_first = lax.ppermute(second_below[:8], "x", UP)
    far_second = lax.ppermute(second_above[8:], "x", DOWN)
    attended, below_b, above_b = lax.optimization_barrier((attended, below_b, above_b))
    attended_full = lax.all_gather(attended, T, axis=1, tiled=True)
    far_first, far_second, attended_full = lax.optimization_barrier(
        (far_first, far_second, attended_full)
    )
    second_mine = jnp.stack(
        [second_set, second_below, jnp.concatenate([far_first, far_second]), second_above]
    ).reshape(64, 32, 512)
    second_theirs = other_core(second_mine)
    moe_both, moe_left, moe_right, mixed_cols, output_block = mix(
        place, everything, attended_full, second_mine, second_theirs, moe_gain
    )

    slot_rank = expert_ranks(column_routes)
    local = column_routes - lax.axis_index("zl") * 16
    group = jnp.arange(4, dtype=jnp.int32)[:, None, None]
    target = jnp.where(
        (local >= 0) & (local < 16), local * (4 * CAP) + group * CAP + slot_rank, -1
    )
    row_ids = jnp.arange(LAYER_ROWS, dtype=jnp.int32)[:, None]
    dispatch = jnp.zeros((LAYER_ROWS, 4 * TOK), F32)
    for k in range(6):
        dispatch = dispatch + (row_ids == target[:, k].reshape(1, 4 * TOK)).astype(F32)
    dispatch = jnp.broadcast_to(dispatch.astype(BF)[None], (2, LAYER_ROWS, 4 * TOK))

    at_zl = lax.axis_index("zl")
    served = (at_zl - rank + 4) % 4
    slots = jnp.arange(16 * 16, dtype=jnp.int32)[:, None]
    back = target - group * CAP
    back = jnp.where(target >= 0, back // (4 * CAP) * 16 + back % (4 * CAP), -1)
    back = lax.dynamic_index_in_dim(back, served, 0, keepdims=False)
    back_gates = lax.dynamic_index_in_dim(column_gates, served, 0, keepdims=False)
    combine = jnp.zeros((16 * 16, TOK), F32)
    for k in range(6):
        combine = combine + jnp.where(slots == back[k][None], back_gates[k][None], 0.0)
    combine = jnp.broadcast_to(combine.astype(BF)[None], (2, 16 * 16, TOK))

    place_ids = jnp.arange(4 * 512, dtype=jnp.int32)
    to_plane, source, slot = place_ids // 512, place_ids // 16 % 32, place_ids % 16
    wanted = source * (4 * CAP) + (at_zl - to_plane + 4) % 4 * CAP + slot
    wanted = jnp.where(slot < CAP, wanted, -1)
    spread = (jnp.arange(2 * LAYER_ROWS, dtype=jnp.int32)[:, None] == wanted[None, :]).astype(BF)

    both_up = jnp.concatenate([expert_gate[0], expert_up[0]], axis=1)
    up_mine = lax.dynamic_slice_in_dim(both_up, core * (D // 2), D // 2, 0)
    up_other = lax.dynamic_slice_in_dim(both_up, (1 - core) * (D // 2), D // 2, 0)

    def rows_by(weight, rows):
        return lax.dot_general(weight, rows, (((0,), (1,)), ((), ())), preferred_element_type=F32)

    at_z = [(z % 4) * 4 + z // 4 for z in range(16)]
    z_up = [(at_z[z], at_z[(z + 1) % 16]) for z in range(16)]
    z_down = [(at_z[z], at_z[(z + 15) % 16]) for z in range(16)]
    back_one = lax.ppermute(moe_both, ("zl", T), z_up)
    on_one = lax.ppermute(moe_both, ("zl", T), z_down)
    far_left = lax.ppermute(moe_left, ("zl", T), [(at_z[z], at_z[(z + 2) % 16]) for z in range(16)])
    far_right = lax.ppermute(
        moe_right, ("zl", T), [(at_z[z], at_z[(z + 14) % 16]) for z in range(16)]
    )
    tokens = jnp.stack(
        [
            jnp.concatenate([moe_left, back_one[:TOK], far_left, on_one[:TOK]]),
            jnp.concatenate([moe_right, back_one[TOK:], far_right, on_one[TOK:]]),
        ]
    )
    outgoing = lax.dot_general(
        dispatch, tokens, (((2,), (1,)), ((0,), (0,))), preferred_element_type=F32
    ).astype(BF)
    below_a, above_a, outgoing = lax.optimization_barrier((below_a, above_a, outgoing))
    down_first = lax.ppermute(below_a, T, UP)
    down_second = lax.ppermute(above_a, T, DOWN)
    mine = lax.all_to_all(
        outgoing.reshape(2 * LAYER_ROWS, D // 2), LAYER, split_axis=0, concat_axis=0, tiled=True
    )
    mine, down_first, down_second = lax.optimization_barrier((mine, down_first, down_second))
    down_far = jnp.concatenate([down_first, down_second])
    theirs = other_core(mine)
    pre = rows_by(up_mine, mine) + rows_by(up_other, theirs)
    own = (jax.nn.silu(pre[:176]) * pre[176:]).astype(BF)
    own = jnp.dot(own, spread, preferred_element_type=F32).astype(BF)
    own = own.reshape(176, 4, 512).transpose(1, 0, 2)
    hidden = lax.all_to_all(own, T, split_axis=0, concat_axis=0, tiled=True).reshape(704, 512)

    down_below = jnp.concatenate([below_a, below_b])
    down_above = jnp.concatenate([above_b, above_a])
    down_all = jnp.stack([down_mine, down_below, down_far, down_above])

    def half_out(half):
        quarters = [
            lax.dynamic_index_in_dim(down_all, (rank + 8 - 2 * half - q) % 4, 0, keepdims=False)
            for q in range(2)
        ]
        return lax.dot_general(
            hidden, jnp.concatenate(quarters, axis=1), (((0,), (0,)), ((), ())),
            preferred_element_type=F32,
        ).astype(BF)

    given = other_core(half_out(1 - core))
    both = (half_out(core).astype(F32) + given.astype(F32)).astype(BF)
    returned = lax.all_to_all(both, LAYER, split_axis=0, concat_axis=0, tiled=True)
    partial = lax.dot_general(
        combine,
        returned.reshape(2, 16 * 16, D // 2),
        (((1,), (1,)), ((0,), (0,))),
        preferred_element_type=F32,
    )
    partial = partial.reshape(2, TOK, 2, 512).transpose(0, 2, 1, 3).reshape(4, TOK, 512)
    total = lax.dynamic_index_in_dim(partial, at_zl, 0, keepdims=False)
    for s in range(1, 4):
        sent = lax.dynamic_index_in_dim(partial, (at_zl + s) % 4, 0, keepdims=False).astype(BF)
        total = total + lax.ppermute(sent, "zl", [(j, (j + s) % 4) for j in range(4)]).astype(F32)
    home = [(a * 4 + b, b * 4 + a) for a in range(4) for b in range(4)]
    sums = lax.ppermute(total.astype(BF), ("zl", T), home)
    result = mixed_cols.astype(F32)
    hidden_out = (result + sums.astype(F32)).astype(BF)
    return (hidden_out, expand_block, output_block, cache_cols)


def solution(mesh):
    fine = Mesh(mesh.devices.reshape(4, 4, 4, 2, 4), DP + (T,))
    rows_both = P(DP + (T,), None)
    in_specs = (
        P(DP, T),
        P(DP, None),
        P(DP, None),
        P(DP, None),
        P(),
        P(),
        P(),
        rows_both,
        rows_both,
        rows_both,
        rows_both,
        P(DP, None, T),
        P(DP, None, T),
        P(DP, None, T),
    )
    out_specs = (P(DP, T), P(None, T), P(None, T), P(DP, T))
    return jax.shard_map(body, mesh=fine, in_specs=in_specs, out_specs=out_specs, check_vma=False)
```

```python
import math

import jax
import jax.numpy as jnp
from jax import lax
from jax.experimental import pallas as pl
from jax.experimental.pallas import tpu as pltpu
from jax.sharding import Mesh
from jax.sharding import PartitionSpec as P

D = 2048
NOPE = 128
ROPE = 64
VDIM = 128
LATENT = 512
EXPERTS = 64
CAP = 14
TOK = 128
LAYER_ROWS = 16 * 4 * CAP

DP = ("zl", "y", "x", "c")
T = "t"
LAYER = ("c", "y", "x")
UP = [(j, (j + 1) % 4) for j in range(4)]
DOWN = [(j, (j + 3) % 4) for j in range(4)]
BF = jnp.bfloat16
F32 = jnp.float32

rope_base = 50000.0


def rms_norm(values, gain_vector):
    mean_square = jnp.mean(values * values, axis=-1, keepdims=True)
    return values * lax.rsqrt(mean_square + 1e-06) * gain_vector


def positions_of(lengths, row_count):
    prompt_ends = jnp.cumsum(lengths, axis=1)
    starts = prompt_ends - lengths
    token_index = jnp.arange(row_count, dtype=jnp.int32)
    segment = jnp.sum(
        (token_index[None, :, None] >= prompt_ends[:, None, :]).astype(jnp.int32), axis=2
    )
    member = segment[:, :, None] == jnp.arange(lengths.shape[1], dtype=jnp.int32)[None, None, :]
    offset = jnp.sum(jnp.where(member, starts[:, None, :], 0), axis=2)
    return (segment, token_index[None, :] - offset)


def expert_ranks(routes):
    experts = jnp.arange(EXPERTS, dtype=jnp.int32)[None, :, None]
    named = [(routes[:, k : k + 1] == experts) for k in range(6)]
    per_token = sum(n.astype(F32) for n in named).astype(BF)
    index = jnp.arange(TOK, dtype=jnp.int32)
    earlier = (index[:, None] < index[None, :]).astype(BF)
    before = lax.dot_general(
        per_token, earlier, (((2,), (0,)), ((), ())), preferred_element_type=F32
    )
    ranks = [jnp.sum(jnp.where(n, before, 0.0), axis=1) for n in named]
    return jnp.stack(ranks, axis=1).astype(jnp.int32)


def shifted(block, axis):
    return [block] + [
        lax.ppermute(block, axis, [(j, (j + s) % 4) for j in range(4)]) for s in range(1, 4)
    ]


def ring(block, axis):
    half = block.shape[0] // 2
    below, above = lax.ppermute(block, axis, UP), lax.ppermute(block, axis, DOWN)
    far = [lax.ppermute(below[:half], axis, UP), lax.ppermute(above[half:], axis, DOWN)]
    return [block, below, jnp.concatenate(far), above]


def other_core(block):
    return lax.ppermute(block, "c", [(0, 1), (1, 0)])


VMEM = pl.BlockSpec(memory_space=pltpu.VMEM)
SMEM = pl.BlockSpec(memory_space=pltpu.SMEM)
NT = (((1,), (1,)), ((), ()))


def pack_rows(query, latent, expand, output, routes, gates):
    def kernel(q_ref, l_ref, e_ref, o_ref, routes_ref, gates_ref, out_ref, rows):
        tail_a, tail_b = l_ref[:, 512:544], l_ref[:, 544:576]
        tail = [tail_a, tail_a, tail_b, tail_b]
        for t in range(4):
            q = q_ref[:, t * 384 : (t + 1) * 384]
            parts = [
                q[:, 0:128], q[:, 192:320],
                q[:, 128:160], q[:, 320:352], q[:, 160:192], q[:, 352:384],
            ]
            rows[t * 4 : t * 4 + 4, :] = jnp.concatenate(parts + tail, axis=1)
            rows[20 + t : 21 + t, :] = e_ref[:, t * 512 : (t + 1) * 512]
        rows[16:20, :] = l_ref[:, 0:512]
        rows[24:28, :] = o_ref[:, 0:512]
        rows[28:32, :] = o_ref[:, 512:1024]
        rows[32:48, :] = jnp.zeros((16, 512), F32)
        rows[32:38, 0:128] = routes_ref[...].astype(F32)
        rows[40:46, 0:128] = gates_ref[...].astype(F32)
        out_ref[...] = rows[...].astype(BF)

    return pl.pallas_call(
        kernel,
        out_shape=jax.ShapeDtypeStruct((48, 512), BF),
        in_specs=[VMEM] * 6,
        out_specs=VMEM,
        scratch_shapes=[pltpu.VMEM((48, 512), F32)],
        name="pack_rows",
    )(query, latent, expand, output, routes.T, gates.T)


def pick_rows(place, everything):
    def kernel(place_ref, in_ref, out_ref, wide, rows):
        t = place_ref[4]
        wide[...] = in_ref[...].astype(F32)
        for s in range(4):
            lanes = slice(s * 512, (s + 1) * 512)
            q = wide[0:4, lanes]
            e = wide[20:21, lanes]
            for k in range(1, 4):
                q = jnp.where(t == k, wide[k * 4 : k * 4 + 4, lanes], q)
                e = jnp.where(t == k, wide[20 + k : 21 + k, lanes], e)
            rows[s * 4 : s * 4 + 4, :] = q
            rows[16 + s * 4 : 20 + s * 4, :] = wide[16:20, lanes]
            rows[32 + s : 33 + s, :] = e
            rows[36 + s : 37 + s, :] = e
            rows[40 + s * 4 : 44 + s * 4, :] = wide[24:28, lanes]
            rows[56 + s * 4 : 60 + s * 4, :] = wide[28:32, lanes]
        out_ref[0] = rows[...].astype(BF)

    return pl.pallas_call(
        kernel,
        grid=(4,),
        out_shape=jax.ShapeDtypeStruct((4, 72, 512), BF),
        in_specs=[SMEM, pl.BlockSpec((32, 2048), lambda i: (0, i))],
        out_specs=pl.BlockSpec((1, 72, 512), lambda i: (i, 0, 0)),
        scratch_shapes=[pltpu.VMEM((32, 2048), F32), pltpu.VMEM((72, 512), F32)],
        name="pick_rows",
    )(place, everything)


def residual(place_ref, parts_ref):
    t = place_ref[4]
    return jnp.concatenate([parts_ref[(t - q + 4) % 4] for q in range(4)], axis=1).astype(F32)


def in_order(place_ref, visit):
    y, x = place_ref[1], place_ref[2]

    def source_of(i):
        row_zl, row_y, row_x = i // 16, (i // 4) % 4, i % 4
        return ((x - row_x + 4) % 4 * 4 + (y - row_y + 4) % 4) * 4 + row_zl

    def step(j, carry):
        visit(j, (source_of(2 * j), source_of(2 * j + 1)))
        return carry

    lax.fori_loop(0, 32, step, 0)


def attention(place, everything, mine, theirs, norm_gain, latent_gain, cosines, sines, allowed):
    def kernel(
        place_ref, in_ref, mine_ref, theirs_ref, norm_ref, gain_ref, cos_ref, sin_ref, allowed_ref,
        attended_ref, latent_ref, rope_ref, expand_ref, q_rows, l_rows,
    ):
        c = place_ref[3]
        low = lax.broadcasted_iota(jnp.int32, (8, 512), 0) < 4

        def visit(j, sources):
            pair = []
            for n, source in enumerate(sources):
                for ref, at in ((mine_ref, c), (theirs_ref, 1 - c)):
                    row = pl.multiple_of(((2 * j + n) * 2 + at) * 16, 16)
                    q_rows[pl.ds(row, 16), :] = ref[source, 0:16, :]
                    l_rows[pl.ds(row, 16), :] = ref[source, 16:32, :]
                own = mine_ref[source, 32:40, :].astype(F32)
                other = theirs_ref[source, 32:40, :].astype(F32)
                first = jnp.where(c == 0, own, other)
                second = jnp.where(c == 0, other, own)
                pair.append(jnp.where(low, first, second))
            row = pl.multiple_of(j * 16, 16)
            expand_ref[pl.ds(row, 16), :] = jnp.concatenate(pair, axis=0).astype(BF)

        in_order(place_ref, visit)
        normed = rms_norm(residual(place_ref, in_ref), norm_ref[...]).astype(BF)
        query = jnp.dot(normed, q_rows[...], preferred_element_type=F32)
        latent = jnp.dot(normed, l_rows[...], preferred_element_type=F32).astype(BF)
        latent = rms_norm(latent.astype(F32), gain_ref[...]).astype(BF)
        latent_ref[...] = latent
        cosine, sine = cos_ref[...], sin_ref[...]

        def rotated(v):
            return (v * cosine + pltpu.roll(v, 64, 1) * sine).astype(BF)

        key_rope = rotated(query[:, 384:512].astype(BF).astype(F32))
        rope_ref[...] = key_rope
        query_rope = rotated(query[:, 256:384])
        expanded = jnp.dot(latent, expand_ref[...], preferred_element_type=F32).astype(BF)
        head_of = (lax.broadcasted_iota(jnp.int32, (128, 128), 1) // 32) % 2
        for h in range(2):
            own_rope = jnp.where(head_of == h, query_rope.astype(F32), 0.0).astype(BF)
            scores = lax.dot_general(
                query[:, h * 128 : (h + 1) * 128].astype(BF),
                expanded[:, h * 256 : h * 256 + 128],
                NT,
                preferred_element_type=F32,
            )
            scores = scores + lax.dot_general(own_rope, key_rope, NT, preferred_element_type=F32)
            scores = scores * (1.0 / math.sqrt(NOPE + ROPE))
            scores = jnp.where(allowed_ref[...] > 0.0, scores, -1e30)
            powers = jnp.exp(scores - jnp.max(scores, axis=-1, keepdims=True))
            probs = (powers / jnp.sum(powers, axis=-1, keepdims=True)).astype(BF)
            out = jnp.dot(
                probs, expanded[:, h * 256 + 128 : h * 256 + 256], preferred_element_type=F32
            )
            attended_ref[:, h * 128 : (h + 1) * 128] = out.astype(BF)

    def whole(*shape):
        return pl.BlockSpec(shape, lambda i: (0,) * len(shape))

    return pl.pallas_call(
        kernel,
        grid=(1,),
        out_shape=[
            jax.ShapeDtypeStruct((128, 256), BF),
            jax.ShapeDtypeStruct((128, 512), BF),
            jax.ShapeDtypeStruct((128, 128), BF),
            jax.ShapeDtypeStruct((512, 512), BF),
        ],
        in_specs=[
            SMEM, whole(4, 128, 512), VMEM, VMEM,
            whole(1, 2048), whole(1, 512), whole(128, 128), whole(128, 128), whole(128, 128),
        ],
        out_specs=[whole(128, 256), whole(128, 512), whole(128, 128), whole(512, 512)],
        scratch_shapes=[pltpu.VMEM((2048, 512), BF), pltpu.VMEM((2048, 512), BF)],
        name="attention",
    )(
        place, everything, mine, theirs, norm_gain.reshape(1, 2048), latent_gain.reshape(1, 512),
        cosines, sines, allowed,
    )


def mix(place, everything, attended, mine, theirs, moe_gain):
    def kernel(
        place_ref, in_ref, attended_ref, mine_ref, theirs_ref, gain_ref,
        moe_ref, cols_ref, server_ref, w_first, w_second,
    ):
        c, t = place_ref[3], place_ref[4]

        def visit(j, sources):
            for n, source in enumerate(sources):
                for ref, at in ((mine_ref, c), (theirs_ref, 1 - c)):
                    row = pl.multiple_of(((2 * j + n) * 2 + at) * 16, 16)
                    first, second = ref[source, 0:16, :], ref[source, 16:32, :]
                    w_first[pl.ds(row, 16), :] = first
                    w_second[pl.ds(row, 16), :] = second
                    half = jnp.where(t < 2, first.astype(F32), second.astype(F32))
                    quarter = jnp.where(t % 2 == 0, half[:, 0:256], half[:, 256:512])
                    server_ref[pl.ds(row, 16), :] = quarter.astype(BF)

        in_order(place_ref, visit)
        total = lax.dot_general(
            attended_ref[:, 0:512], w_first[...], NT, preferred_element_type=F32
        ) + lax.dot_general(
            attended_ref[:, 512:1024], w_second[...], NT, preferred_element_type=F32
        )
        mixed = (residual(place_ref, in_ref) + total).astype(BF).astype(F32)
        cols = mixed[:, 0:512]
        for k in range(1, 4):
            cols = jnp.where(t == k, mixed[:, k * 512 : (k + 1) * 512], cols)
        cols_ref[...] = cols.astype(BF)
        moe = rms_norm(mixed, gain_ref[...]).astype(BF)
        moe_ref[0:128, :] = moe[:, 0:1024]
        moe_ref[128:256, :] = moe[:, 1024:2048]

    def whole(*shape):
        return pl.BlockSpec(shape, lambda i: (0,) * len(shape))

    return pl.pallas_call(
        kernel,
        grid=(1,),
        out_shape=[
            jax.ShapeDtypeStruct((256, 1024), BF),
            jax.ShapeDtypeStruct((128, 512), BF),
            jax.ShapeDtypeStruct((2048, 256), BF),
        ],
        in_specs=[SMEM, whole(4, 128, 512), whole(128, 1024), VMEM, VMEM, whole(1, 2048)],
        out_specs=[whole(256, 1024), whole(128, 512), whole(2048, 256)],
        scratch_shapes=[pltpu.VMEM((2048, 512), BF), pltpu.VMEM((2048, 512), BF)],
        name="mix",
    )(place, everything, attended, mine, theirs, moe_gain.reshape(1, 2048))


def body(
    hidden_in,
    lengths,
    routes,
    gate_weights,
    norm_gain,
    latent_gain,
    moe_gain,
    query_train,
    latent_train,
    expand_train,
    output_train,
    expert_gate,
    expert_up,
    expert_down,
):
    rank = lax.axis_index(T)
    core = lax.axis_index("c")
    place = jnp.stack([lax.axis_index(a) for a in DP + (T,)]).astype(jnp.int32)

    packed = pack_rows(
        query_train, latent_train, expand_train, output_train, routes, gate_weights
    )
    everything = lax.all_gather(packed, ("zl", T), axis=1, tiled=True)
    picked = pick_rows(place, everything)
    meta = everything[32:48].reshape(16, 4, 2048)[:, :, 0:128].transpose(1, 0, 2)
    at_zl = lax.axis_index("zl")
    meta = jnp.stack(
        [lax.dynamic_index_in_dim(meta, (at_zl - s + 4) % 4, 0, keepdims=False) for s in range(4)]
    )
    column_routes = meta[:, 0:6].astype(jnp.int32)
    column_gates = meta[:, 8:14].astype(F32)
    gathered = jnp.stack(shifted(picked, "y")).reshape(16, 72, 512)
    hidden_gated, _ = lax.optimization_barrier((hidden_in, picked))
    hidden_parts = shifted(hidden_gated, T)
    gathered, *hidden_parts = lax.optimization_barrier((gathered, *hidden_parts))
    hidden_parts = jnp.stack(hidden_parts)
    first_set = gathered[:, :40]
    first_mine = jnp.stack(ring(first_set, "x")).reshape(64, 40, 512)
    first_theirs = other_core(first_mine)
    second_set, _ = lax.optimization_barrier((gathered[:, 40:], first_theirs))
    second_below = lax.ppermute(second_set, "x", UP)
    second_above = lax.ppermute(second_set, "x", DOWN)

    segment, position = positions_of(lengths, TOK)
    segment = segment[0]
    frequency = jnp.exp(jnp.arange(32, dtype=F32) * (-2.0 * math.log(rope_base) / 64))
    angles = position[0].astype(F32)[:, None] * frequency[None, :]
    cosine, sine = jnp.cos(angles), jnp.sin(angles)
    token_index = jnp.arange(TOK, dtype=jnp.int32)
    allowed = (segment[:, None] == segment[None, :]) & (token_index[None, :] <= token_index[:, None])
    attended, latent_normed, key_rope, expand_block = attention(
        place,
        hidden_parts,
        first_mine,
        first_theirs,
        norm_gain,
        latent_gain,
        jnp.concatenate([cosine] * 4, axis=1),
        jnp.concatenate([-sine, -sine, sine, sine], axis=1),
        allowed.astype(F32),
    )
    cache_full = jnp.concatenate([latent_normed, key_rope[:, 0:32], key_rope[:, 64:96]], axis=1)
    cache_cols = lax.dynamic_slice_in_dim(cache_full, rank * 144, 144, 1)
    second_below, second_above, attended = lax.optimization_barrier(
        (second_below, second_above, attended)
    )
    far_first = lax.ppermute(second_below[:8], "x", UP)
    far_second = lax.ppermute(second_above[8:], "x", DOWN)
    attended_full = lax.all_gather(attended, T, axis=1, tiled=True)
    far_first, far_second, attended_full = lax.optimization_barrier(
        (far_first, far_second, attended_full)
    )
    second_mine = jnp.stack(
        [second_set, second_below, jnp.concatenate([far_first, far_second]), second_above]
    ).reshape(64, 32, 512)
    second_theirs = other_core(second_mine)
    moe_halves, mixed_cols, output_block = mix(
        place, hidden_parts, attended_full, second_mine, second_theirs, moe_gain
    )

    slot_rank = expert_ranks(column_routes)
    local = column_routes - at_zl * 16
    group = jnp.arange(4, dtype=jnp.int32)[:, None, None]
    target = jnp.where(
        (local >= 0) & (local < 16), local * (4 * CAP) + group * CAP + slot_rank, -1
    )
    row_ids = jnp.arange(LAYER_ROWS, dtype=jnp.int32)[:, None]
    dispatch = jnp.zeros((LAYER_ROWS, 4 * TOK), F32)
    combine = jnp.zeros((LAYER_ROWS, 4 * TOK), F32)
    for k in range(6):
        hit = row_ids == target[:, k].reshape(1, 4 * TOK)
        dispatch = dispatch + hit.astype(F32)
        combine = combine + jnp.where(hit, column_gates[:, k].reshape(1, 4 * TOK), 0.0)
    dispatch = jnp.broadcast_to(dispatch.astype(BF)[None], (2, LAYER_ROWS, 4 * TOK))
    combine = jnp.broadcast_to(combine.astype(BF)[None], (2, LAYER_ROWS, 4 * TOK))

    def halves(matrix):
        return (
            lax.dynamic_slice_in_dim(matrix, core * (D // 2), D // 2, 0),
            lax.dynamic_slice_in_dim(matrix, (1 - core) * (D // 2), D // 2, 0),
        )

    gate_mine, gate_other = halves(expert_gate[0])
    up_mine, up_other = halves(expert_up[0])
    around = [(rank + 4 - back) % 4 for back in (0, 1, 3, 2)]
    down_around = jnp.concatenate(
        [lax.dynamic_slice_in_dim(expert_down[0], at * 176, 176, 0) for at in around], axis=0
    )

    def rows_by(weight, rows):
        return lax.dot_general(weight, rows, (((0,), (1,)), ((), ())), preferred_element_type=F32)

    at_z = [(z % 4) * 4 + z // 4 for z in range(16)]
    z_up = [(at_z[z], at_z[(z + 1) % 16]) for z in range(16)]
    z_down = [(at_z[z], at_z[(z + 15) % 16]) for z in range(16)]
    back_one = lax.ppermute(moe_halves, ("zl", T), z_up)
    on_one = lax.ppermute(moe_halves, ("zl", T), z_down)
    far_left = lax.ppermute(back_one[:TOK], ("zl", T), z_up)
    far_right = lax.ppermute(on_one[TOK:], ("zl", T), z_down)
    tokens = jnp.stack(
        [
            jnp.concatenate([moe_halves[:TOK], back_one[:TOK], far_left, on_one[:TOK]]),
            jnp.concatenate([moe_halves[TOK:], back_one[TOK:], far_right, on_one[TOK:]]),
        ]
    )
    outgoing = lax.dot_general(
        dispatch, tokens, (((2,), (1,)), ((0,), (0,))), preferred_element_type=F32
    ).astype(BF)
    mine = lax.all_to_all(
        outgoing.reshape(2 * LAYER_ROWS, D // 2), LAYER, split_axis=0, concat_axis=0, tiled=True
    )
    theirs = other_core(mine)
    gate_part = rows_by(gate_mine, mine) + rows_by(gate_other, theirs)
    up_part = rows_by(up_mine, mine) + rows_by(up_other, theirs)
    own = (jax.nn.silu(gate_part) * up_part).astype(BF)

    below = lax.ppermute(own, T, UP)
    above = lax.ppermute(own, T, DOWN)
    far_first = lax.ppermute(below[:88], T, UP)
    far_second = lax.ppermute(above[88:], T, DOWN)

    def out_of(pieces, at):
        rows = jnp.concatenate(pieces, axis=0)
        return lax.dot_general(
            rows, down_around[at : at + rows.shape[0]], (((0,), (0,)), ((), ())),
            preferred_element_type=F32,
        )

    half_out = (out_of([own, below, above], 0) + out_of([far_first, far_second], 528)).astype(BF)
    keep = lax.dynamic_slice_in_dim(half_out, core * 256, 256, 1)
    give = lax.dynamic_slice_in_dim(half_out, (1 - core) * 256, 256, 1)
    both = (keep.astype(F32) + other_core(give).astype(F32)).astype(BF)
    returned = lax.all_to_all(both, LAYER, split_axis=0, concat_axis=0, tiled=True)
    partial = lax.dot_general(
        combine,
        returned.reshape(2, LAYER_ROWS, 256),
        (((1,), (1,)), ((0,), (0,))),
        preferred_element_type=F32,
    ).reshape(2, 4, TOK, 256)
    sums = partial[:, 0]
    for s in range(1, 4):
        sent = partial[:, s].astype(BF)
        sums = sums + lax.ppermute(sent, "zl", [(j, (j - s) % 4) for j in range(4)]).astype(F32)
    result = mixed_cols.astype(F32)
    hidden_out = (result + jnp.concatenate([sums[0], sums[1]], axis=1)).astype(BF)
    return (hidden_out, expand_block, output_block, cache_cols)


def solution(mesh):
    fine = Mesh(mesh.devices.reshape(4, 4, 4, 2, 4), DP + (T,))
    rows_both = P(DP + (T,), None)
    in_specs = (
        P(DP, T),
        P(DP, None),
        P(DP, None),
        P(DP, None),
        P(),
        P(),
        P(),
        rows_both,
        rows_both,
        rows_both,
        rows_both,
        P(DP, None, T),
        P(DP, None, T),
        P(DP, None, T),
    )
    out_specs = (P(DP, T), P(None, T), P(None, T), P(DP, T))
    return jax.shard_map(body, mesh=fine, in_specs=in_specs, out_specs=out_specs, check_vma=False)
```

```python
import math

import jax
import jax.numpy as jnp
from jax import lax
from jax.experimental import pallas as pl
from jax.experimental.pallas import tpu as pltpu
from jax.sharding import Mesh
from jax.sharding import PartitionSpec as P

D = 2048
NOPE = 128
ROPE = 64
VDIM = 128
LATENT = 512
EXPERTS = 64
CAP = 14
TOK = 128
LAYER_ROWS = 16 * 4 * CAP

DP = ("zl", "y", "x", "c")
T = "t"
LAYER = ("c", "y", "x")
UP = [(j, (j + 1) % 4) for j in range(4)]
DOWN = [(j, (j + 3) % 4) for j in range(4)]
BF = jnp.bfloat16
F32 = jnp.float32

rope_base = 50000.0


def rms_norm(values, gain_vector):
    mean_square = jnp.mean(values * values, axis=-1, keepdims=True)
    return values * lax.rsqrt(mean_square + 1e-06) * gain_vector


def positions_of(lengths, row_count):
    prompt_ends = jnp.cumsum(lengths, axis=1)
    starts = prompt_ends - lengths
    token_index = jnp.arange(row_count, dtype=jnp.int32)
    segment = jnp.sum(
        (token_index[None, :, None] >= prompt_ends[:, None, :]).astype(jnp.int32), axis=2
    )
    member = segment[:, :, None] == jnp.arange(lengths.shape[1], dtype=jnp.int32)[None, None, :]
    offset = jnp.sum(jnp.where(member, starts[:, None, :], 0), axis=2)
    return (segment, token_index[None, :] - offset)


def expert_ranks(routes):
    experts = jnp.arange(EXPERTS, dtype=jnp.int32)[None, :, None]
    named = [(routes[:, k : k + 1] == experts) for k in range(6)]
    per_token = sum(n.astype(F32) for n in named).astype(BF)
    index = jnp.arange(TOK, dtype=jnp.int32)
    earlier = (index[:, None] < index[None, :]).astype(BF)
    before = lax.dot_general(
        per_token, earlier, (((2,), (0,)), ((), ())), preferred_element_type=F32
    )
    ranks = [jnp.sum(jnp.where(n, before, 0.0), axis=1) for n in named]
    return jnp.stack(ranks, axis=1).astype(jnp.int32)


def shifted(block, axis):
    return [block] + [
        lax.ppermute(block, axis, [(j, (j + s) % 4) for j in range(4)]) for s in range(1, 4)
    ]


def ring(block, axis):
    half = block.shape[0] // 2
    below, above = lax.ppermute(block, axis, UP), lax.ppermute(block, axis, DOWN)
    far = [lax.ppermute(below[:half], axis, UP), lax.ppermute(above[half:], axis, DOWN)]
    return [block, below, jnp.concatenate(far), above]


def other_core(block):
    return lax.ppermute(block, "c", [(0, 1), (1, 0)])


VMEM = pl.BlockSpec(memory_space=pltpu.VMEM)
SMEM = pl.BlockSpec(memory_space=pltpu.SMEM)
NT = (((1,), (1,)), ((), ()))


def pack_rows(hidden_in, query, latent, expand, output):
    def kernel(hidden_ref, q_ref, l_ref, e_ref, o_ref, out_ref, rows):
        out_ref[0:128, :] = hidden_ref[...]
        tail_a, tail_b = l_ref[:, 512:544], l_ref[:, 544:576]
        tail = [tail_a, tail_a, tail_b, tail_b]
        for t in range(4):
            q = q_ref[:, t * 384 : (t + 1) * 384]
            parts = [
                q[:, 0:128], q[:, 192:320],
                q[:, 128:160], q[:, 320:352], q[:, 160:192], q[:, 352:384],
            ]
            rows[t * 4 : t * 4 + 4, :] = jnp.concatenate(parts + tail, axis=1)
            rows[20 + t : 21 + t, :] = e_ref[:, t * 512 : (t + 1) * 512]
        rows[16:20, :] = l_ref[:, 0:512]
        rows[24:28, :] = o_ref[:, 0:512]
        rows[28:32, :] = o_ref[:, 512:1024]
        out_ref[128:160, :] = rows[...].astype(BF)

    return pl.pallas_call(
        kernel,
        out_shape=jax.ShapeDtypeStruct((160, 512), BF),
        in_specs=[VMEM] * 5,
        out_specs=VMEM,
        scratch_shapes=[pltpu.VMEM((32, 512), F32)],
        name="pack_rows",
    )(hidden_in, query, latent, expand, output)


def pick_rows(place, everything, routes, gates):
    def kernel(place_ref, in_ref, routes_ref, gates_ref, out_ref, wide, rows):
        t = place_ref[4]
        wide[...] = in_ref[...].astype(F32)
        for s in range(4):
            lanes = slice(s * 512, (s + 1) * 512)
            q = wide[0:4, lanes]
            e = wide[20:21, lanes]
            for k in range(1, 4):
                q = jnp.where(t == k, wide[k * 4 : k * 4 + 4, lanes], q)
                e = jnp.where(t == k, wide[20 + k : 21 + k, lanes], e)
            rows[s * 4 : s * 4 + 4, :] = q
            rows[16 + s * 4 : 20 + s * 4, :] = wide[16:20, lanes]
            rows[32 + s : 33 + s, :] = e
            rows[36 + s : 37 + s, :] = e
            rows[40 + s * 4 : 44 + s * 4, :] = wide[24:28, lanes]
            rows[56 + s * 4 : 60 + s * 4, :] = wide[28:32, lanes]
        rows[72:88, :] = jnp.zeros((16, 512), F32)
        rows[72:78, 0:128] = routes_ref[...].astype(F32)
        rows[80:86, 0:128] = gates_ref[...].astype(F32)
        out_ref[...] = rows[...].astype(BF)

    def small(rows):
        return pl.BlockSpec((rows, 128), lambda i: (0, 0))

    return pl.pallas_call(
        kernel,
        grid=(1,),
        out_shape=jax.ShapeDtypeStruct((88, 512), BF),
        in_specs=[SMEM, pl.BlockSpec((32, 2048), lambda i: (4, 0)), small(6), small(6)],
        out_specs=pl.BlockSpec((88, 512), lambda i: (0, 0)),
        scratch_shapes=[pltpu.VMEM((32, 2048), F32), pltpu.VMEM((88, 512), F32)],
        name="pick_rows",
    )(place, everything, routes.T, gates.T)


def in_order(place_ref, visit):
    zl, y, x = place_ref[0], place_ref[1], place_ref[2]

    def source_of(i):
        row_zl, row_y, row_x = i // 16, (i // 4) % 4, i % 4
        return ((x - row_x + 4) % 4 * 4 + (y - row_y + 4) % 4) * 4 + (zl - row_zl + 4) % 4

    def step(j, carry):
        visit(j, (source_of(2 * j), source_of(2 * j + 1)))
        return carry

    lax.fori_loop(0, 32, step, 0)


def attention(place, everything, mine, theirs, norm_gain, latent_gain, cosines, sines, allowed):
    def kernel(
        place_ref, in_ref, mine_ref, theirs_ref, norm_ref, gain_ref, cos_ref, sin_ref, allowed_ref,
        attended_ref, latent_ref, rope_ref, expand_ref, q_rows, l_rows,
    ):
        c = place_ref[3]
        low = lax.broadcasted_iota(jnp.int32, (8, 512), 0) < 4

        def visit(j, sources):
            pair = []
            for n, source in enumerate(sources):
                for ref, at in ((mine_ref, c), (theirs_ref, 1 - c)):
                    row = pl.multiple_of(((2 * j + n) * 2 + at) * 16, 16)
                    q_rows[pl.ds(row, 16), :] = ref[source, 0:16, :]
                    l_rows[pl.ds(row, 16), :] = ref[source, 16:32, :]
                own = mine_ref[source, 32:40, :].astype(F32)
                other = theirs_ref[source, 32:40, :].astype(F32)
                first = jnp.where(c == 0, own, other)
                second = jnp.where(c == 0, other, own)
                pair.append(jnp.where(low, first, second))
            row = pl.multiple_of(j * 16, 16)
            expand_ref[pl.ds(row, 16), :] = jnp.concatenate(pair, axis=0).astype(BF)

        in_order(place_ref, visit)
        normed = rms_norm(in_ref[...].astype(F32), norm_ref[...]).astype(BF)
        query = jnp.dot(normed, q_rows[...], preferred_element_type=F32)
        latent = jnp.dot(normed, l_rows[...], preferred_element_type=F32).astype(BF)
        latent = rms_norm(latent.astype(F32), gain_ref[...]).astype(BF)
        latent_ref[...] = latent
        cosine, sine = cos_ref[...], sin_ref[...]

        def rotated(v):
            return (v * cosine + pltpu.roll(v, 64, 1) * sine).astype(BF)

        key_rope = rotated(query[:, 384:512].astype(BF).astype(F32))
        rope_ref[...] = key_rope
        query_rope = rotated(query[:, 256:384])
        expanded = jnp.dot(latent, expand_ref[...], preferred_element_type=F32).astype(BF)
        head_of = (lax.broadcasted_iota(jnp.int32, (128, 128), 1) // 32) % 2
        for h in range(2):
            own_rope = jnp.where(head_of == h, query_rope.astype(F32), 0.0).astype(BF)
            scores = lax.dot_general(
                query[:, h * 128 : (h + 1) * 128].astype(BF),
                expanded[:, h * 256 : h * 256 + 128],
                NT,
                preferred_element_type=F32,
            )
            scores = scores + lax.dot_general(own_rope, key_rope, NT, preferred_element_type=F32)
            scores = scores * (1.0 / math.sqrt(NOPE + ROPE))
            scores = jnp.where(allowed_ref[...] > 0.0, scores, -1e30)
            powers = jnp.exp(scores - jnp.max(scores, axis=-1, keepdims=True))
            probs = (powers / jnp.sum(powers, axis=-1, keepdims=True)).astype(BF)
            out = jnp.dot(
                probs, expanded[:, h * 256 + 128 : h * 256 + 256], preferred_element_type=F32
            )
            attended_ref[:, h * 128 : (h + 1) * 128] = out.astype(BF)

    def whole(*shape):
        return pl.BlockSpec(shape, lambda i: (0,) * len(shape))

    return pl.pallas_call(
        kernel,
        grid=(1,),
        out_shape=[
            jax.ShapeDtypeStruct((128, 256), BF),
            jax.ShapeDtypeStruct((128, 512), BF),
            jax.ShapeDtypeStruct((128, 128), BF),
            jax.ShapeDtypeStruct((512, 512), BF),
        ],
        in_specs=[
            SMEM, whole(128, 2048), VMEM, VMEM,
            whole(1, 2048), whole(1, 512), whole(128, 128), whole(128, 128), whole(128, 128),
        ],
        out_specs=[whole(128, 256), whole(128, 512), whole(128, 128), whole(512, 512)],
        scratch_shapes=[pltpu.VMEM((2048, 512), BF), pltpu.VMEM((2048, 512), BF)],
        name="attention",
    )(
        place, everything, mine, theirs, norm_gain.reshape(1, 2048), latent_gain.reshape(1, 512),
        cosines, sines, allowed,
    )


def mix(place, everything, attended, mine, theirs, moe_gain):
    def kernel(
        place_ref, in_ref, attended_ref, mine_ref, theirs_ref, gain_ref,
        moe_ref, cols_ref, server_ref, w_first, w_second,
    ):
        c, t = place_ref[3], place_ref[4]

        def visit(j, sources):
            for n, source in enumerate(sources):
                for ref, at in ((mine_ref, c), (theirs_ref, 1 - c)):
                    row = pl.multiple_of(((2 * j + n) * 2 + at) * 16, 16)
                    first, second = ref[source, 0:16, :], ref[source, 16:32, :]
                    w_first[pl.ds(row, 16), :] = first
                    w_second[pl.ds(row, 16), :] = second
                    half = jnp.where(t < 2, first.astype(F32), second.astype(F32))
                    quarter = jnp.where(t % 2 == 0, half[:, 0:256], half[:, 256:512])
                    server_ref[pl.ds(row, 16), :] = quarter.astype(BF)

        in_order(place_ref, visit)
        total = lax.dot_general(
            attended_ref[:, 0:512], w_first[...], NT, preferred_element_type=F32
        ) + lax.dot_general(
            attended_ref[:, 512:1024], w_second[...], NT, preferred_element_type=F32
        )
        mixed = (in_ref[...].astype(F32) + total).astype(BF).astype(F32)
        cols = mixed[:, 0:512]
        for k in range(1, 4):
            cols = jnp.where(t == k, mixed[:, k * 512 : (k + 1) * 512], cols)
        cols_ref[...] = cols.astype(BF)
        moe = rms_norm(mixed, gain_ref[...]).astype(BF)
        moe_ref[0:128, :] = moe[:, 0:1024]
        moe_ref[128:256, :] = moe[:, 1024:2048]

    def whole(*shape):
        return pl.BlockSpec(shape, lambda i: (0,) * len(shape))

    return pl.pallas_call(
        kernel,
        grid=(1,),
        out_shape=[
            jax.ShapeDtypeStruct((256, 1024), BF),
            jax.ShapeDtypeStruct((128, 512), BF),
            jax.ShapeDtypeStruct((2048, 256), BF),
        ],
        in_specs=[SMEM, whole(128, 2048), whole(128, 1024), VMEM, VMEM, whole(1, 2048)],
        out_specs=[whole(256, 1024), whole(128, 512), whole(2048, 256)],
        scratch_shapes=[pltpu.VMEM((2048, 512), BF), pltpu.VMEM((2048, 512), BF)],
        name="mix",
    )(place, everything, attended, mine, theirs, moe_gain.reshape(1, 2048))


def body(
    hidden_in,
    lengths,
    routes,
    gate_weights,
    norm_gain,
    latent_gain,
    moe_gain,
    query_train,
    latent_train,
    expand_train,
    output_train,
    expert_gate,
    expert_up,
    expert_down,
):
    rank = lax.axis_index(T)
    core = lax.axis_index("c")
    place = jnp.stack([lax.axis_index(a) for a in DP + (T,)]).astype(jnp.int32)

    packed = pack_rows(hidden_in, query_train, latent_train, expand_train, output_train)
    everything = lax.all_gather(packed, T, axis=1, tiled=True)
    rows = pick_rows(place, everything, routes, gate_weights)
    gathered = jnp.stack(shifted(rows, "zl"))
    column_routes = gathered[:, 72:78, 0:128].astype(jnp.int32)
    column_gates = gathered[:, 80:86, 0:128].astype(F32)
    gathered = jnp.stack(shifted(gathered[:, :72], "y")).reshape(16, 72, 512)
    first_set = gathered[:, :40]
    first_mine = jnp.stack(ring(first_set, "x")).reshape(64, 40, 512)
    first_theirs = other_core(first_mine)
    second_set, _ = lax.optimization_barrier((gathered[:, 40:], first_theirs))
    second_parts = shifted(second_set, "x")

    segment, position = positions_of(lengths, TOK)
    segment = segment[0]
    frequency = jnp.exp(jnp.arange(32, dtype=F32) * (-2.0 * math.log(rope_base) / 64))
    angles = position[0].astype(F32)[:, None] * frequency[None, :]
    cosine, sine = jnp.cos(angles), jnp.sin(angles)
    token_index = jnp.arange(TOK, dtype=jnp.int32)
    allowed = (segment[:, None] == segment[None, :]) & (token_index[None, :] <= token_index[:, None])
    attended, latent_normed, key_rope, expand_block = attention(
        place,
        everything,
        first_mine,
        first_theirs,
        norm_gain,
        latent_gain,
        jnp.concatenate([cosine] * 4, axis=1),
        jnp.concatenate([-sine, -sine, sine, sine], axis=1),
        allowed.astype(F32),
    )
    cache_full = jnp.concatenate([latent_normed, key_rope[:, 0:32], key_rope[:, 64:96]], axis=1)
    cache_cols = lax.dynamic_slice_in_dim(cache_full, rank * 144, 144, 1)
    attended_full = lax.all_gather(attended, T, axis=1, tiled=True)
    attended_full, *second_parts = lax.optimization_barrier((attended_full, *second_parts))
    second_mine = jnp.stack(second_parts).reshape(64, 32, 512)
    second_theirs = other_core(second_mine)
    moe_halves, mixed_cols, output_block = mix(
        place, everything, attended_full, second_mine, second_theirs, moe_gain
    )

    slot_rank = expert_ranks(column_routes)
    local = column_routes - lax.axis_index("zl") * 16
    group = jnp.arange(4, dtype=jnp.int32)[:, None, None]
    target = jnp.where(
        (local >= 0) & (local < 16), local * (4 * CAP) + group * CAP + slot_rank, -1
    )
    row_ids = jnp.arange(LAYER_ROWS, dtype=jnp.int32)[:, None]
    dispatch = jnp.zeros((LAYER_ROWS, 4 * TOK), F32)
    combine = jnp.zeros((LAYER_ROWS, 4 * TOK), F32)
    for k in range(6):
        hit = row_ids == target[:, k].reshape(1, 4 * TOK)
        dispatch = dispatch + hit.astype(F32)
        combine = combine + jnp.where(hit, column_gates[:, k].reshape(1, 4 * TOK), 0.0)
    dispatch = jnp.broadcast_to(dispatch.astype(BF)[None], (2, LAYER_ROWS, 4 * TOK))
    combine = jnp.broadcast_to(combine.astype(BF)[None], (2, LAYER_ROWS, 4 * TOK))

    def halves(matrix):
        return (
            lax.dynamic_slice_in_dim(matrix, core * (D // 2), D // 2, 0),
            lax.dynamic_slice_in_dim(matrix, (1 - core) * (D // 2), D // 2, 0),
        )

    gate_mine, gate_other = halves(expert_gate[0])
    up_mine, up_other = halves(expert_up[0])
    around = [(rank + 4 - back) % 4 for back in (0, 1, 3, 2)]
    down_around = jnp.concatenate(
        [lax.dynamic_slice_in_dim(expert_down[0], at * 176, 176, 0) for at in around], axis=0
    )

    def rows_by(weight, rows):
        return lax.dot_general(weight, rows, (((0,), (1,)), ((), ())), preferred_element_type=F32)

    at_z = [(z % 4) * 4 + z // 4 for z in range(16)]
    z_up = [(at_z[z], at_z[(z + 1) % 16]) for z in range(16)]
    z_down = [(at_z[z], at_z[(z + 15) % 16]) for z in range(16)]
    back_one = lax.ppermute(moe_halves, ("zl", T), z_up)
    on_one = lax.ppermute(moe_halves, ("zl", T), z_down)
    far_left = lax.ppermute(back_one[:TOK], ("zl", T), z_up)
    far_right = lax.ppermute(on_one[TOK:], ("zl", T), z_down)
    tokens = jnp.stack(
        [
            jnp.concatenate([moe_halves[:TOK], back_one[:TOK], far_left, on_one[:TOK]]),
            jnp.concatenate([moe_halves[TOK:], back_one[TOK:], far_right, on_one[TOK:]]),
        ]
    )
    outgoing = lax.dot_general(
        dispatch, tokens, (((2,), (1,)), ((0,), (0,))), preferred_element_type=F32
    ).astype(BF)
    mine = lax.all_to_all(
        outgoing.reshape(2 * LAYER_ROWS, D // 2), LAYER, split_axis=0, concat_axis=0, tiled=True
    )
    theirs = other_core(mine)
    gate_part = rows_by(gate_mine, mine) + rows_by(gate_other, theirs)
    up_part = rows_by(up_mine, mine) + rows_by(up_other, theirs)
    own = (jax.nn.silu(gate_part) * up_part).astype(BF)

    below = lax.ppermute(own, T, UP)
    above = lax.ppermute(own, T, DOWN)
    far_first = lax.ppermute(below[:88], T, UP)
    far_second = lax.ppermute(above[88:], T, DOWN)

    def out_of(pieces, at):
        rows = jnp.concatenate(pieces, axis=0)
        return lax.dot_general(
            rows, down_around[at : at + rows.shape[0]], (((0,), (0,)), ((), ())),
            preferred_element_type=F32,
        )

    half_out = (out_of([own, below, above], 0) + out_of([far_first, far_second], 528)).astype(BF)
    keep = lax.dynamic_slice_in_dim(half_out, core * 256, 256, 1)
    give = lax.dynamic_slice_in_dim(half_out, (1 - core) * 256, 256, 1)
    both = (keep.astype(F32) + other_core(give).astype(F32)).astype(BF)
    returned = lax.all_to_all(both, LAYER, split_axis=0, concat_axis=0, tiled=True)
    partial = lax.dot_general(
        combine,
        returned.reshape(2, LAYER_ROWS, 256),
        (((1,), (1,)), ((0,), (0,))),
        preferred_element_type=F32,
    ).reshape(2, 4, TOK, 256)
    sums = partial[:, 0]
    for s in range(1, 4):
        sent = partial[:, s].astype(BF)
        sums = sums + lax.ppermute(sent, "zl", [(j, (j - s) % 4) for j in range(4)]).astype(F32)
    result = mixed_cols.astype(F32)
    hidden_out = (result + jnp.concatenate([sums[0], sums[1]], axis=1)).astype(BF)
    return (hidden_out, expand_block, output_block, cache_cols)


def solution(mesh):
    fine = Mesh(mesh.devices.reshape(4, 4, 4, 2, 4), DP + (T,))
    rows_both = P(DP + (T,), None)
    in_specs = (
        P(DP, T),
        P(DP, None),
        P(DP, None),
        P(DP, None),
        P(),
        P(),
        P(),
        rows_both,
        rows_both,
        rows_both,
        rows_both,
        P(DP, None, T),
        P(DP, None, T),
        P(DP, None, T),
    )
    out_specs = (P(DP, T), P(None, T), P(None, T), P(DP, T))
    return jax.shard_map(body, mesh=fine, in_specs=in_specs, out_specs=out_specs, check_vma=False)
```

```python
import math

import jax
import jax.numpy as jnp
from jax import lax
from jax.experimental import pallas as pl
from jax.experimental.pallas import tpu as pltpu
from jax.sharding import Mesh
from jax.sharding import PartitionSpec as P

D = 2048
NOPE = 128
ROPE = 64
VDIM = 128
LATENT = 512
EXPERTS = 64
CAP = 14
TOK = 128
LAYER_ROWS = 16 * 4 * CAP

DP = ("zl", "y", "x", "c")
T = "t"
LAYER = ("c", "y", "x")
UP = [(j, (j + 1) % 4) for j in range(4)]
DOWN = [(j, (j + 3) % 4) for j in range(4)]
BF = jnp.bfloat16
F32 = jnp.float32

rope_base = 50000.0


def rms_norm(values, gain_vector):
    mean_square = jnp.mean(values * values, axis=-1, keepdims=True)
    return values * lax.rsqrt(mean_square + 1e-06) * gain_vector


def positions_of(lengths, row_count):
    prompt_ends = jnp.cumsum(lengths, axis=1)
    starts = prompt_ends - lengths
    token_index = jnp.arange(row_count, dtype=jnp.int32)
    segment = jnp.sum(
        (token_index[None, :, None] >= prompt_ends[:, None, :]).astype(jnp.int32), axis=2
    )
    member = segment[:, :, None] == jnp.arange(lengths.shape[1], dtype=jnp.int32)[None, None, :]
    offset = jnp.sum(jnp.where(member, starts[:, None, :], 0), axis=2)
    return (segment, token_index[None, :] - offset)


def expert_ranks(routes):
    experts = jnp.arange(EXPERTS, dtype=jnp.int32)[None, :, None]
    named = [(routes[:, k : k + 1] == experts) for k in range(6)]
    per_token = sum(n.astype(F32) for n in named).astype(BF)
    index = jnp.arange(TOK, dtype=jnp.int32)
    earlier = (index[:, None] < index[None, :]).astype(BF)
    before = lax.dot_general(
        per_token, earlier, (((2,), (0,)), ((), ())), preferred_element_type=F32
    )
    ranks = [jnp.sum(jnp.where(n, before, 0.0), axis=1) for n in named]
    return jnp.stack(ranks, axis=1).astype(jnp.int32)


def shifted(block, axis):
    return [block] + [
        lax.ppermute(block, axis, [(j, (j + s) % 4) for j in range(4)]) for s in range(1, 4)
    ]


def ring(block, axis):
    half = block.shape[0] // 2
    below, above = lax.ppermute(block, axis, UP), lax.ppermute(block, axis, DOWN)
    far = [lax.ppermute(below[:half], axis, UP), lax.ppermute(above[half:], axis, DOWN)]
    return [block, below, jnp.concatenate(far), above]


def other_core(block):
    return lax.ppermute(block, "c", [(0, 1), (1, 0)])


VMEM = pl.BlockSpec(memory_space=pltpu.VMEM)
SMEM = pl.BlockSpec(memory_space=pltpu.SMEM)
NT = (((1,), (1,)), ((), ()))


def pack_rows(hidden_in, query, latent, expand, output):
    def kernel(hidden_ref, q_ref, l_ref, e_ref, o_ref, out_ref, rows):
        out_ref[0:128, :] = hidden_ref[...]
        tail_a, tail_b = l_ref[:, 512:544], l_ref[:, 544:576]
        tail = [tail_a, tail_a, tail_b, tail_b]
        for t in range(4):
            q = q_ref[:, t * 384 : (t + 1) * 384]
            parts = [
                q[:, 0:128], q[:, 192:320],
                q[:, 128:160], q[:, 320:352], q[:, 160:192], q[:, 352:384],
            ]
            rows[t * 4 : t * 4 + 4, :] = jnp.concatenate(parts + tail, axis=1)
            rows[20 + t : 21 + t, :] = e_ref[:, t * 512 : (t + 1) * 512]
        rows[16:20, :] = l_ref[:, 0:512]
        rows[24:28, :] = o_ref[:, 0:512]
        rows[28:32, :] = o_ref[:, 512:1024]
        out_ref[128:160, :] = rows[...].astype(BF)

    return pl.pallas_call(
        kernel,
        out_shape=jax.ShapeDtypeStruct((160, 512), BF),
        in_specs=[VMEM] * 5,
        out_specs=VMEM,
        scratch_shapes=[pltpu.VMEM((32, 512), F32)],
        name="pack_rows",
    )(hidden_in, query, latent, expand, output)


def pick_rows(place, everything, routes, gates):
    def kernel(place_ref, in_ref, routes_ref, gates_ref, out_ref, wide, rows):
        t = place_ref[4]
        wide[...] = in_ref[...].astype(F32)
        for s in range(4):
            lanes = slice(s * 512, (s + 1) * 512)
            q = wide[0:4, lanes]
            e = wide[20:21, lanes]
            for k in range(1, 4):
                q = jnp.where(t == k, wide[k * 4 : k * 4 + 4, lanes], q)
                e = jnp.where(t == k, wide[20 + k : 21 + k, lanes], e)
            rows[s * 4 : s * 4 + 4, :] = q
            rows[16 + s * 4 : 20 + s * 4, :] = wide[16:20, lanes]
            rows[32 + s : 33 + s, :] = e
            rows[36 + s : 37 + s, :] = e
            rows[40 + s * 4 : 44 + s * 4, :] = wide[24:28, lanes]
            rows[56 + s * 4 : 60 + s * 4, :] = wide[28:32, lanes]
        rows[72:88, :] = jnp.zeros((16, 512), F32)
        rows[72:78, 0:128] = routes_ref[...].astype(F32)
        rows[80:86, 0:128] = gates_ref[...].astype(F32)
        out_ref[...] = rows[...].astype(BF)

    def small(rows):
        return pl.BlockSpec((rows, 128), lambda i: (0, 0))

    return pl.pallas_call(
        kernel,
        grid=(1,),
        out_shape=jax.ShapeDtypeStruct((88, 512), BF),
        in_specs=[SMEM, pl.BlockSpec((32, 2048), lambda i: (4, 0)), small(6), small(6)],
        out_specs=pl.BlockSpec((88, 512), lambda i: (0, 0)),
        scratch_shapes=[pltpu.VMEM((32, 2048), F32), pltpu.VMEM((88, 512), F32)],
        name="pick_rows",
    )(place, everything, routes.T, gates.T)


def in_order(place_ref, visit):
    zl, y, x = place_ref[0], place_ref[1], place_ref[2]

    def source_of(i):
        row_zl, row_y, row_x = i // 16, (i // 4) % 4, i % 4
        return ((x - row_x + 4) % 4 * 4 + (y - row_y + 4) % 4) * 4 + (zl - row_zl + 4) % 4

    def step(j, carry):
        visit(j, (source_of(2 * j), source_of(2 * j + 1)))
        return carry

    lax.fori_loop(0, 32, step, 0)


def attention(place, everything, mine, theirs, norm_gain, latent_gain, cosines, sines, allowed):
    def kernel(
        place_ref, in_ref, mine_ref, theirs_ref, norm_ref, gain_ref, cos_ref, sin_ref, allowed_ref,
        attended_ref, latent_ref, rope_ref, expand_ref, q_rows, l_rows,
    ):
        c = place_ref[3]
        low = lax.broadcasted_iota(jnp.int32, (8, 512), 0) < 4

        def visit(j, sources):
            pair = []
            for n, source in enumerate(sources):
                for ref, at in ((mine_ref, c), (theirs_ref, 1 - c)):
                    row = pl.multiple_of(((2 * j + n) * 2 + at) * 16, 16)
                    q_rows[pl.ds(row, 16), :] = ref[source, 0:16, :]
                    l_rows[pl.ds(row, 16), :] = ref[source, 16:32, :]
                own = mine_ref[source, 32:40, :].astype(F32)
                other = theirs_ref[source, 32:40, :].astype(F32)
                first = jnp.where(c == 0, own, other)
                second = jnp.where(c == 0, other, own)
                pair.append(jnp.where(low, first, second))
            row = pl.multiple_of(j * 16, 16)
            expand_ref[pl.ds(row, 16), :] = jnp.concatenate(pair, axis=0).astype(BF)

        in_order(place_ref, visit)
        normed = rms_norm(in_ref[...].astype(F32), norm_ref[...]).astype(BF)
        query = jnp.dot(normed, q_rows[...], preferred_element_type=F32)
        latent = jnp.dot(normed, l_rows[...], preferred_element_type=F32).astype(BF)
        latent = rms_norm(latent.astype(F32), gain_ref[...]).astype(BF)
        latent_ref[...] = latent
        cosine, sine = cos_ref[...], sin_ref[...]

        def rotated(v):
            return (v * cosine + pltpu.roll(v, 64, 1) * sine).astype(BF)

        key_rope = rotated(query[:, 384:512].astype(BF).astype(F32))
        rope_ref[...] = key_rope
        query_rope = rotated(query[:, 256:384])
        expanded = jnp.dot(latent, expand_ref[...], preferred_element_type=F32).astype(BF)
        head_of = (lax.broadcasted_iota(jnp.int32, (128, 128), 1) // 32) % 2
        for h in range(2):
            own_rope = jnp.where(head_of == h, query_rope.astype(F32), 0.0).astype(BF)
            scores = lax.dot_general(
                query[:, h * 128 : (h + 1) * 128].astype(BF),
                expanded[:, h * 256 : h * 256 + 128],
                NT,
                preferred_element_type=F32,
            )
            scores = scores + lax.dot_general(own_rope, key_rope, NT, preferred_element_type=F32)
            scores = scores * (1.0 / math.sqrt(NOPE + ROPE))
            scores = jnp.where(allowed_ref[...] > 0.0, scores, -1e30)
            powers = jnp.exp(scores - jnp.max(scores, axis=-1, keepdims=True))
            probs = (powers / jnp.sum(powers, axis=-1, keepdims=True)).astype(BF)
            out = jnp.dot(
                probs, expanded[:, h * 256 + 128 : h * 256 + 256], preferred_element_type=F32
            )
            attended_ref[:, h * 128 : (h + 1) * 128] = out.astype(BF)

    def whole(*shape):
        return pl.BlockSpec(shape, lambda i: (0,) * len(shape))

    return pl.pallas_call(
        kernel,
        grid=(1,),
        out_shape=[
            jax.ShapeDtypeStruct((128, 256), BF),
            jax.ShapeDtypeStruct((128, 512), BF),
            jax.ShapeDtypeStruct((128, 128), BF),
            jax.ShapeDtypeStruct((512, 512), BF),
        ],
        in_specs=[
            SMEM, whole(128, 2048), VMEM, VMEM,
            whole(1, 2048), whole(1, 512), whole(128, 128), whole(128, 128), whole(128, 128),
        ],
        out_specs=[whole(128, 256), whole(128, 512), whole(128, 128), whole(512, 512)],
        scratch_shapes=[pltpu.VMEM((2048, 512), BF), pltpu.VMEM((2048, 512), BF)],
        name="attention",
    )(
        place, everything, mine, theirs, norm_gain.reshape(1, 2048), latent_gain.reshape(1, 512),
        cosines, sines, allowed,
    )


def mix(place, everything, attended, mine, theirs, moe_gain):
    def kernel(
        place_ref, in_ref, attended_ref, mine_ref, theirs_ref, gain_ref,
        left_ref, right_ref, cols_ref, server_ref, w_first, w_second,
    ):
        c, t = place_ref[3], place_ref[4]

        def visit(j, sources):
            for n, source in enumerate(sources):
                for ref, at in ((mine_ref, c), (theirs_ref, 1 - c)):
                    row = pl.multiple_of(((2 * j + n) * 2 + at) * 16, 16)
                    first, second = ref[source, 0:16, :], ref[source, 16:32, :]
                    w_first[pl.ds(row, 16), :] = first
                    w_second[pl.ds(row, 16), :] = second
                    half = jnp.where(t < 2, first.astype(F32), second.astype(F32))
                    quarter = jnp.where(t % 2 == 0, half[:, 0:256], half[:, 256:512])
                    server_ref[pl.ds(row, 16), :] = quarter.astype(BF)

        in_order(place_ref, visit)
        total = lax.dot_general(
            attended_ref[:, 0:512], w_first[...], NT, preferred_element_type=F32
        ) + lax.dot_general(
            attended_ref[:, 512:1024], w_second[...], NT, preferred_element_type=F32
        )
        mixed = (in_ref[...].astype(F32) + total).astype(BF).astype(F32)
        cols = mixed[:, 0:512]
        for k in range(1, 4):
            cols = jnp.where(t == k, mixed[:, k * 512 : (k + 1) * 512], cols)
        cols_ref[...] = cols.astype(BF)
        moe = rms_norm(mixed, gain_ref[...]).astype(BF)
        left_ref[...] = moe[:, 0:1024]
        right_ref[...] = moe[:, 1024:2048]

    def whole(*shape):
        return pl.BlockSpec(shape, lambda i: (0,) * len(shape))

    return pl.pallas_call(
        kernel,
        grid=(1,),
        out_shape=[
            jax.ShapeDtypeStruct((128, 1024), BF),
            jax.ShapeDtypeStruct((128, 1024), BF),
            jax.ShapeDtypeStruct((128, 512), BF),
            jax.ShapeDtypeStruct((2048, 256), BF),
        ],
        in_specs=[SMEM, whole(128, 2048), whole(128, 1024), VMEM, VMEM, whole(1, 2048)],
        out_specs=[whole(128, 1024), whole(128, 1024), whole(128, 512), whole(2048, 256)],
        scratch_shapes=[pltpu.VMEM((2048, 512), BF), pltpu.VMEM((2048, 512), BF)],
        name="mix",
    )(place, everything, attended, mine, theirs, moe_gain.reshape(1, 2048))


def body(
    hidden_in,
    lengths,
    routes,
    gate_weights,
    norm_gain,
    latent_gain,
    moe_gain,
    query_train,
    latent_train,
    expand_train,
    output_train,
    expert_gate,
    expert_up,
    expert_down,
):
    rank = lax.axis_index(T)
    core = lax.axis_index("c")
    place = jnp.stack([lax.axis_index(a) for a in DP + (T,)]).astype(jnp.int32)

    packed = pack_rows(hidden_in, query_train, latent_train, expand_train, output_train)
    everything = lax.all_gather(packed, T, axis=1, tiled=True)
    rows = pick_rows(place, everything, routes, gate_weights)
    gathered = jnp.stack(shifted(rows, "zl"))
    column_routes = gathered[:, 72:78, 0:128].astype(jnp.int32)
    column_gates = gathered[:, 80:86, 0:128].astype(F32)
    gathered = jnp.stack(shifted(gathered[:, :72], "y")).reshape(16, 72, 512)
    first_set = gathered[:, :40]
    first_mine = jnp.stack(ring(first_set, "x")).reshape(64, 40, 512)
    first_theirs = other_core(first_mine)
    second_set, _ = lax.optimization_barrier((gathered[:, 40:], first_theirs))
    second_parts = shifted(second_set, "x")

    segment, position = positions_of(lengths, TOK)
    segment = segment[0]
    frequency = jnp.exp(jnp.arange(32, dtype=F32) * (-2.0 * math.log(rope_base) / 64))
    angles = position[0].astype(F32)[:, None] * frequency[None, :]
    cosine, sine = jnp.cos(angles), jnp.sin(angles)
    token_index = jnp.arange(TOK, dtype=jnp.int32)
    allowed = (segment[:, None] == segment[None, :]) & (token_index[None, :] <= token_index[:, None])
    attended, latent_normed, key_rope, expand_block = attention(
        place,
        everything,
        first_mine,
        first_theirs,
        norm_gain,
        latent_gain,
        jnp.concatenate([cosine] * 4, axis=1),
        jnp.concatenate([-sine, -sine, sine, sine], axis=1),
        allowed.astype(F32),
    )
    cache_full = jnp.concatenate([latent_normed, key_rope[:, 0:32], key_rope[:, 64:96]], axis=1)
    cache_cols = lax.dynamic_slice_in_dim(cache_full, rank * 144, 144, 1)
    attended_full = lax.all_gather(attended, T, axis=1, tiled=True)
    attended_full, *second_parts = lax.optimization_barrier((attended_full, *second_parts))
    second_mine = jnp.stack(second_parts).reshape(64, 32, 512)
    second_theirs = other_core(second_mine)
    left, right, mixed_cols, output_block = mix(
        place, everything, attended_full, second_mine, second_theirs, moe_gain
    )

    slot_rank = expert_ranks(column_routes)
    local = column_routes - lax.axis_index("zl") * 16
    group = jnp.arange(4, dtype=jnp.int32)[:, None, None]
    target = jnp.where(
        (local >= 0) & (local < 16), local * (4 * CAP) + group * CAP + slot_rank, -1
    )
    row_ids = jnp.arange(LAYER_ROWS, dtype=jnp.int32)[:, None]
    dispatch = jnp.zeros((LAYER_ROWS, 4 * TOK), F32)
    combine = jnp.zeros((LAYER_ROWS, 4 * TOK), F32)
    for k in range(6):
        hit = row_ids == target[:, k].reshape(1, 4 * TOK)
        dispatch = dispatch + hit.astype(F32)
        combine = combine + jnp.where(hit, column_gates[:, k].reshape(1, 4 * TOK), 0.0)
    dispatch = jnp.broadcast_to(dispatch.astype(BF)[None], (2, LAYER_ROWS, 4 * TOK))
    combine = jnp.broadcast_to(combine.astype(BF)[None], (2, LAYER_ROWS, 4 * TOK))

    def halves(matrix):
        return (
            lax.dynamic_slice_in_dim(matrix, core * (D // 2), D // 2, 0),
            lax.dynamic_slice_in_dim(matrix, (1 - core) * (D // 2), D // 2, 0),
        )

    gate_mine, gate_other = halves(expert_gate[0])
    up_mine, up_other = halves(expert_up[0])
    around = [(rank + 4 - back) % 4 for back in (0, 1, 3, 2)]
    down_around = jnp.concatenate(
        [lax.dynamic_slice_in_dim(expert_down[0], at * 176, 176, 0) for at in around], axis=0
    )

    def rows_by(weight, rows):
        return lax.dot_general(weight, rows, (((0,), (1,)), ((), ())), preferred_element_type=F32)

    at_z = [(z % 4) * 4 + z // 4 for z in range(16)]
    z_up = [(at_z[z], at_z[(z + 1) % 16]) for z in range(16)]
    z_down = [(at_z[z], at_z[(z + 15) % 16]) for z in range(16)]
    back_left = lax.ppermute(left, ("zl", T), z_up)
    on_right = lax.ppermute(right, ("zl", T), z_down)
    back_right = lax.ppermute(right, ("zl", T), z_up)
    on_left = lax.ppermute(left, ("zl", T), z_down)
    far_left = lax.ppermute(back_left, ("zl", T), z_up)
    far_right = lax.ppermute(on_right, ("zl", T), z_down)
    tokens = jnp.stack(
        [
            jnp.concatenate([left, back_left, far_left, on_left]),
            jnp.concatenate([right, back_right, far_right, on_right]),
        ]
    )
    outgoing = lax.dot_general(
        dispatch, tokens, (((2,), (1,)), ((0,), (0,))), preferred_element_type=F32
    ).astype(BF)
    mine = lax.all_to_all(
        outgoing.reshape(2 * LAYER_ROWS, D // 2), LAYER, split_axis=0, concat_axis=0, tiled=True
    )
    theirs = other_core(mine)
    gate_part = rows_by(gate_mine, mine) + rows_by(gate_other, theirs)
    up_part = rows_by(up_mine, mine) + rows_by(up_other, theirs)
    own = (jax.nn.silu(gate_part) * up_part).astype(BF)

    first, second = own[:88], own[88:]
    below_first = lax.ppermute(first, T, UP)
    above_second = lax.ppermute(second, T, DOWN)
    below_second = lax.ppermute(second, T, UP)
    above_first = lax.ppermute(first, T, DOWN)
    far_first = lax.ppermute(below_first, T, UP)
    far_second = lax.ppermute(above_second, T, DOWN)

    def out_of(pieces, at):
        rows = jnp.concatenate(pieces, axis=0)
        return lax.dot_general(
            rows, down_around[at : at + rows.shape[0]], (((0,), (0,)), ((), ())),
            preferred_element_type=F32,
        )

    half_out = (out_of([own, below_first, below_second, above_first, above_second], 0) + out_of([far_first, far_second], 528)).astype(BF)
    keep = lax.dynamic_slice_in_dim(half_out, core * 256, 256, 1)
    give = lax.dynamic_slice_in_dim(half_out, (1 - core) * 256, 256, 1)
    both = (keep.astype(F32) + other_core(give).astype(F32)).astype(BF)
    returned = lax.all_to_all(both, LAYER, split_axis=0, concat_axis=0, tiled=True)
    partial = lax.dot_general(
        combine,
        returned.reshape(2, LAYER_ROWS, 256),
        (((1,), (1,)), ((0,), (0,))),
        preferred_element_type=F32,
    ).reshape(2, 4, TOK, 256)
    sums = partial[:, 0]
    for s in range(1, 4):
        sent = partial[:, s].astype(BF)
        sums = sums + lax.ppermute(sent, "zl", [(j, (j - s) % 4) for j in range(4)]).astype(F32)
    result = mixed_cols.astype(F32)
    hidden_out = (result + jnp.concatenate([sums[0], sums[1]], axis=1)).astype(BF)
    return (hidden_out, expand_block, output_block, cache_cols)


def solution(mesh):
    fine = Mesh(mesh.devices.reshape(4, 4, 4, 2, 4), DP + (T,))
    rows_both = P(DP + (T,), None)
    in_specs = (
        P(DP, T),
        P(DP, None),
        P(DP, None),
        P(DP, None),
        P(),
        P(),
        P(),
        rows_both,
        rows_both,
        rows_both,
        rows_both,
        P(DP, None, T),
        P(DP, None, T),
        P(DP, None, T),
    )
    out_specs = (P(DP, T), P(None, T), P(None, T), P(DP, T))
    return jax.shard_map(body, mesh=fine, in_specs=in_specs, out_specs=out_specs, check_vma=False)
```

```python
import math

import jax
import jax.numpy as jnp
from jax import lax
from jax.experimental import pallas as pl
from jax.experimental.pallas import tpu as pltpu
from jax.sharding import Mesh
from jax.sharding import PartitionSpec as P

D = 2048
NOPE = 128
ROPE = 64
VDIM = 128
LATENT = 512
EXPERTS = 64
CAP = 14
TOK = 128
LAYER_ROWS = 16 * 4 * CAP

DP = ("zl", "y", "x", "c")
T = "t"
LAYER = ("c", "y", "x")
UP = [(j, (j + 1) % 4) for j in range(4)]
DOWN = [(j, (j + 3) % 4) for j in range(4)]
BF = jnp.bfloat16
F32 = jnp.float32

rope_base = 50000.0


def rms_norm(values, gain_vector):
    mean_square = jnp.mean(values * values, axis=-1, keepdims=True)
    return values * lax.rsqrt(mean_square + 1e-06) * gain_vector


def positions_of(lengths, row_count):
    prompt_ends = jnp.cumsum(lengths, axis=1)
    starts = prompt_ends - lengths
    token_index = jnp.arange(row_count, dtype=jnp.int32)
    segment = jnp.sum(
        (token_index[None, :, None] >= prompt_ends[:, None, :]).astype(jnp.int32), axis=2
    )
    member = segment[:, :, None] == jnp.arange(lengths.shape[1], dtype=jnp.int32)[None, None, :]
    offset = jnp.sum(jnp.where(member, starts[:, None, :], 0), axis=2)
    return (segment, token_index[None, :] - offset)


def expert_ranks(routes):
    experts = jnp.arange(EXPERTS, dtype=jnp.int32)[None, :, None]
    named = [(routes[:, k : k + 1] == experts) for k in range(6)]
    per_token = sum(n.astype(F32) for n in named).astype(BF)
    index = jnp.arange(TOK, dtype=jnp.int32)
    earlier = (index[:, None] < index[None, :]).astype(BF)
    before = lax.dot_general(
        per_token, earlier, (((2,), (0,)), ((), ())), preferred_element_type=F32
    )
    ranks = [jnp.sum(jnp.where(n, before, 0.0), axis=1) for n in named]
    return jnp.stack(ranks, axis=1).astype(jnp.int32)


def shifted(block, axis):
    return [block] + [
        lax.ppermute(block, axis, [(j, (j + s) % 4) for j in range(4)]) for s in range(1, 4)
    ]


def ring(block, axis):
    half = block.shape[0] // 2
    below, above = lax.ppermute(block, axis, UP), lax.ppermute(block, axis, DOWN)
    far = [lax.ppermute(below[:half], axis, UP), lax.ppermute(above[half:], axis, DOWN)]
    return [block, below, jnp.concatenate(far), above]


def other_core(block):
    return lax.ppermute(block, "c", [(0, 1), (1, 0)])


VMEM = pl.BlockSpec(memory_space=pltpu.VMEM)
SMEM = pl.BlockSpec(memory_space=pltpu.SMEM)
NT = (((1,), (1,)), ((), ()))


def pack_rows(hidden_in, query, latent, expand, output):
    def kernel(hidden_ref, q_ref, l_ref, e_ref, o_ref, out_ref, rows):
        out_ref[0:128, :] = hidden_ref[...]
        tail_a, tail_b = l_ref[:, 512:544], l_ref[:, 544:576]
        tail = [tail_a, tail_a, tail_b, tail_b]
        for t in range(4):
            q = q_ref[:, t * 384 : (t + 1) * 384]
            parts = [
                q[:, 0:128], q[:, 192:320],
                q[:, 128:160], q[:, 320:352], q[:, 160:192], q[:, 352:384],
            ]
            rows[t * 4 : t * 4 + 4, :] = jnp.concatenate(parts + tail, axis=1)
            rows[20 + t : 21 + t, :] = e_ref[:, t * 512 : (t + 1) * 512]
        rows[16:20, :] = l_ref[:, 0:512]
        rows[24:28, :] = o_ref[:, 0:512]
        rows[28:32, :] = o_ref[:, 512:1024]
        out_ref[128:160, :] = rows[...].astype(BF)

    return pl.pallas_call(
        kernel,
        out_shape=jax.ShapeDtypeStruct((160, 512), BF),
        in_specs=[VMEM] * 5,
        out_specs=VMEM,
        scratch_shapes=[pltpu.VMEM((32, 512), F32)],
        name="pack_rows",
    )(hidden_in, query, latent, expand, output)


def pick_rows(place, everything, routes, gates):
    def kernel(place_ref, in_ref, routes_ref, gates_ref, out_ref, wide, rows):
        t = place_ref[4]
        wide[...] = in_ref[...].astype(F32)
        for s in range(4):
            lanes = slice(s * 512, (s + 1) * 512)
            q = wide[0:4, lanes]
            e = wide[20:21, lanes]
            for k in range(1, 4):
                q = jnp.where(t == k, wide[k * 4 : k * 4 + 4, lanes], q)
                e = jnp.where(t == k, wide[20 + k : 21 + k, lanes], e)
            rows[s * 4 : s * 4 + 4, :] = q
            rows[16 + s * 4 : 20 + s * 4, :] = wide[16:20, lanes]
            rows[32 + s : 33 + s, :] = e
            rows[36 + s : 37 + s, :] = e
            rows[40 + s * 4 : 44 + s * 4, :] = wide[24:28, lanes]
            rows[56 + s * 4 : 60 + s * 4, :] = wide[28:32, lanes]
        rows[72:88, :] = jnp.zeros((16, 512), F32)
        rows[72:78, 0:128] = routes_ref[...].astype(F32)
        rows[80:86, 0:128] = gates_ref[...].astype(F32)
        out_ref[...] = rows[...].astype(BF)

    def small(rows):
        return pl.BlockSpec((rows, 128), lambda i: (0, 0))

    return pl.pallas_call(
        kernel,
        grid=(1,),
        out_shape=jax.ShapeDtypeStruct((88, 512), BF),
        in_specs=[SMEM, pl.BlockSpec((32, 2048), lambda i: (4, 0)), small(6), small(6)],
        out_specs=pl.BlockSpec((88, 512), lambda i: (0, 0)),
        scratch_shapes=[pltpu.VMEM((32, 2048), F32), pltpu.VMEM((88, 512), F32)],
        name="pick_rows",
    )(place, everything, routes.T, gates.T)


def in_order(place_ref, visit):
    zl, y, x = place_ref[0], place_ref[1], place_ref[2]

    def source_of(i):
        row_zl, row_y, row_x = i // 16, (i // 4) % 4, i % 4
        return ((x - row_x + 4) % 4 * 4 + (y - row_y + 4) % 4) * 4 + (zl - row_zl + 4) % 4

    def step(j, carry):
        visit(j, (source_of(2 * j), source_of(2 * j + 1)))
        return carry

    lax.fori_loop(0, 32, step, 0)


def attention(place, everything, mine, theirs, norm_gain, latent_gain, cosines, sines, allowed):
    def kernel(
        place_ref, in_ref, mine_ref, theirs_ref, norm_ref, gain_ref, cos_ref, sin_ref, allowed_ref,
        attended_ref, latent_ref, rope_ref, expand_ref, q_rows, l_rows,
    ):
        c = place_ref[3]
        low = lax.broadcasted_iota(jnp.int32, (8, 512), 0) < 4

        def visit(j, sources):
            pair = []
            for n, source in enumerate(sources):
                for ref, at in ((mine_ref, c), (theirs_ref, 1 - c)):
                    row = pl.multiple_of(((2 * j + n) * 2 + at) * 16, 16)
                    q_rows[pl.ds(row, 16), :] = ref[source, 0:16, :]
                    l_rows[pl.ds(row, 16), :] = ref[source, 16:32, :]
                own = mine_ref[source, 32:40, :].astype(F32)
                other = theirs_ref[source, 32:40, :].astype(F32)
                first = jnp.where(c == 0, own, other)
                second = jnp.where(c == 0, other, own)
                pair.append(jnp.where(low, first, second))
            row = pl.multiple_of(j * 16, 16)
            expand_ref[pl.ds(row, 16), :] = jnp.concatenate(pair, axis=0).astype(BF)

        in_order(place_ref, visit)
        normed = rms_norm(in_ref[...].astype(F32), norm_ref[...]).astype(BF)
        query = jnp.dot(normed, q_rows[...], preferred_element_type=F32)
        latent = jnp.dot(normed, l_rows[...], preferred_element_type=F32).astype(BF)
        latent = rms_norm(latent.astype(F32), gain_ref[...]).astype(BF)
        latent_ref[...] = latent
        cosine, sine = cos_ref[...], sin_ref[...]

        def rotated(v):
            return (v * cosine + pltpu.roll(v, 64, 1) * sine).astype(BF)

        key_rope = rotated(query[:, 384:512].astype(BF).astype(F32))
        rope_ref[...] = key_rope
        query_rope = rotated(query[:, 256:384])
        expanded = jnp.dot(latent, expand_ref[...], preferred_element_type=F32).astype(BF)
        head_of = (lax.broadcasted_iota(jnp.int32, (128, 128), 1) // 32) % 2
        for h in range(2):
            own_rope = jnp.where(head_of == h, query_rope.astype(F32), 0.0).astype(BF)
            scores = lax.dot_general(
                query[:, h * 128 : (h + 1) * 128].astype(BF),
                expanded[:, h * 256 : h * 256 + 128],
                NT,
                preferred_element_type=F32,
            )
            scores = scores + lax.dot_general(own_rope, key_rope, NT, preferred_element_type=F32)
            scores = scores * (1.0 / math.sqrt(NOPE + ROPE))
            scores = jnp.where(allowed_ref[...] > 0.0, scores, -1e30)
            powers = jnp.exp(scores - jnp.max(scores, axis=-1, keepdims=True))
            probs = (powers / jnp.sum(powers, axis=-1, keepdims=True)).astype(BF)
            out = jnp.dot(
                probs, expanded[:, h * 256 + 128 : h * 256 + 256], preferred_element_type=F32
            )
            attended_ref[:, h * 128 : (h + 1) * 128] = out.astype(BF)

    def whole(*shape):
        return pl.BlockSpec(shape, lambda i: (0,) * len(shape))

    return pl.pallas_call(
        kernel,
        grid=(1,),
        out_shape=[
            jax.ShapeDtypeStruct((128, 256), BF),
            jax.ShapeDtypeStruct((128, 512), BF),
            jax.ShapeDtypeStruct((128, 128), BF),
            jax.ShapeDtypeStruct((512, 512), BF),
        ],
        in_specs=[
            SMEM, whole(128, 2048), VMEM, VMEM,
            whole(1, 2048), whole(1, 512), whole(128, 128), whole(128, 128), whole(128, 128),
        ],
        out_specs=[whole(128, 256), whole(128, 512), whole(128, 128), whole(512, 512)],
        scratch_shapes=[pltpu.VMEM((2048, 512), BF), pltpu.VMEM((2048, 512), BF)],
        name="attention",
    )(
        place, everything, mine, theirs, norm_gain.reshape(1, 2048), latent_gain.reshape(1, 512),
        cosines, sines, allowed,
    )


def mix(place, everything, attended, mine, theirs, moe_gain):
    def kernel(
        place_ref, in_ref, attended_ref, mine_ref, theirs_ref, gain_ref,
        left_ref, right_ref, cols_ref, server_ref, w_first, w_second,
    ):
        c, t = place_ref[3], place_ref[4]

        def visit(j, sources):
            for n, source in enumerate(sources):
                for ref, at in ((mine_ref, c), (theirs_ref, 1 - c)):
                    row = pl.multiple_of(((2 * j + n) * 2 + at) * 16, 16)
                    first, second = ref[source, 0:16, :], ref[source, 16:32, :]
                    w_first[pl.ds(row, 16), :] = first
                    w_second[pl.ds(row, 16), :] = second
                    half = jnp.where(t < 2, first.astype(F32), second.astype(F32))
                    quarter = jnp.where(t % 2 == 0, half[:, 0:256], half[:, 256:512])
                    server_ref[pl.ds(row, 16), :] = quarter.astype(BF)

        in_order(place_ref, visit)
        total = lax.dot_general(
            attended_ref[:, 0:512], w_first[...], NT, preferred_element_type=F32
        ) + lax.dot_general(
            attended_ref[:, 512:1024], w_second[...], NT, preferred_element_type=F32
        )
        mixed = (in_ref[...].astype(F32) + total).astype(BF).astype(F32)
        cols = mixed[:, 0:512]
        for k in range(1, 4):
            cols = jnp.where(t == k, mixed[:, k * 512 : (k + 1) * 512], cols)
        cols_ref[...] = cols.astype(BF)
        moe = rms_norm(mixed, gain_ref[...]).astype(BF)
        left_ref[...] = moe[:, 0:1024]
        right_ref[...] = moe[:, 1024:2048]

    def whole(*shape):
        return pl.BlockSpec(shape, lambda i: (0,) * len(shape))

    return pl.pallas_call(
        kernel,
        grid=(1,),
        out_shape=[
            jax.ShapeDtypeStruct((128, 1024), BF),
            jax.ShapeDtypeStruct((128, 1024), BF),
            jax.ShapeDtypeStruct((128, 512), BF),
            jax.ShapeDtypeStruct((2048, 256), BF),
        ],
        in_specs=[SMEM, whole(128, 2048), whole(128, 1024), VMEM, VMEM, whole(1, 2048)],
        out_specs=[whole(128, 1024), whole(128, 1024), whole(128, 512), whole(2048, 256)],
        scratch_shapes=[pltpu.VMEM((2048, 512), BF), pltpu.VMEM((2048, 512), BF)],
        name="mix",
    )(place, everything, attended, mine, theirs, moe_gain.reshape(1, 2048))


def body(
    hidden_in,
    lengths,
    routes,
    gate_weights,
    norm_gain,
    latent_gain,
    moe_gain,
    query_train,
    latent_train,
    expand_train,
    output_train,
    expert_gate,
    expert_up,
    expert_down,
):
    rank = lax.axis_index(T)
    core = lax.axis_index("c")
    place = jnp.stack([lax.axis_index(a) for a in DP + (T,)]).astype(jnp.int32)

    packed = pack_rows(hidden_in, query_train, latent_train, expand_train, output_train)
    everything = lax.all_gather(packed, T, axis=1, tiled=True)
    rows = pick_rows(place, everything, routes, gate_weights)
    gathered = jnp.stack(shifted(rows, "zl"))
    column_routes = gathered[:, 72:78, 0:128].astype(jnp.int32)
    column_gates = gathered[:, 80:86, 0:128].astype(F32)
    gathered = jnp.stack(shifted(gathered[:, :72], "y")).reshape(16, 72, 512)
    first_set = gathered[:, :40]
    first_mine = jnp.stack(ring(first_set, "x")).reshape(64, 40, 512)
    first_theirs = other_core(first_mine)
    second_set, _ = lax.optimization_barrier((gathered[:, 40:], first_theirs))
    second_parts = shifted(second_set, "x")

    segment, position = positions_of(lengths, TOK)
    segment = segment[0]
    frequency = jnp.exp(jnp.arange(32, dtype=F32) * (-2.0 * math.log(rope_base) / 64))
    angles = position[0].astype(F32)[:, None] * frequency[None, :]
    cosine, sine = jnp.cos(angles), jnp.sin(angles)
    token_index = jnp.arange(TOK, dtype=jnp.int32)
    allowed = (segment[:, None] == segment[None, :]) & (token_index[None, :] <= token_index[:, None])
    attended, latent_normed, key_rope, expand_block = attention(
        place,
        everything,
        first_mine,
        first_theirs,
        norm_gain,
        latent_gain,
        jnp.concatenate([cosine] * 4, axis=1),
        jnp.concatenate([-sine, -sine, sine, sine], axis=1),
        allowed.astype(F32),
    )
    cache_full = jnp.concatenate([latent_normed, key_rope[:, 0:32], key_rope[:, 64:96]], axis=1)
    cache_cols = lax.dynamic_slice_in_dim(cache_full, rank * 144, 144, 1)
    attended_full = lax.all_gather(attended, T, axis=1, tiled=True)
    attended_full, *second_parts = lax.optimization_barrier((attended_full, *second_parts))
    second_mine = jnp.stack(second_parts).reshape(64, 32, 512)
    second_theirs = other_core(second_mine)
    left, right, mixed_cols, output_block = mix(
        place, everything, attended_full, second_mine, second_theirs, moe_gain
    )

    slot_rank = expert_ranks(column_routes)
    local = column_routes - lax.axis_index("zl") * 16
    group = jnp.arange(4, dtype=jnp.int32)[:, None, None]
    target = jnp.where(
        (local >= 0) & (local < 16), local * (4 * CAP) + group * CAP + slot_rank, -1
    )
    row_ids = jnp.arange(LAYER_ROWS, dtype=jnp.int32)[:, None]
    dispatch = jnp.zeros((LAYER_ROWS, 4 * TOK), F32)
    combine = jnp.zeros((LAYER_ROWS, 4 * TOK), F32)
    for k in range(6):
        hit = row_ids == target[:, k].reshape(1, 4 * TOK)
        dispatch = dispatch + hit.astype(F32)
        combine = combine + jnp.where(hit, column_gates[:, k].reshape(1, 4 * TOK), 0.0)
    dispatch = jnp.broadcast_to(dispatch.astype(BF)[None], (2, LAYER_ROWS, 4 * TOK))
    combine = jnp.broadcast_to(combine.astype(BF)[None], (2, LAYER_ROWS, 4 * TOK))

    def halves(matrix):
        return (
            lax.dynamic_slice_in_dim(matrix, core * (D // 2), D // 2, 0),
            lax.dynamic_slice_in_dim(matrix, (1 - core) * (D // 2), D // 2, 0),
        )

    gate_mine, gate_other = halves(expert_gate[0])
    up_mine, up_other = halves(expert_up[0])
    around = [(rank + 4 - back) % 4 for back in (0, 1, 3, 2)]
    down_around = jnp.concatenate(
        [lax.dynamic_slice_in_dim(expert_down[0], at * 176, 176, 0) for at in around], axis=0
    )

    def rows_by(weight, rows):
        return lax.dot_general(weight, rows, (((0,), (1,)), ((), ())), preferred_element_type=F32)

    at_z = [(z % 4) * 4 + z // 4 for z in range(16)]
    z_up = [(at_z[z], at_z[(z + 1) % 16]) for z in range(16)]
    z_down = [(at_z[z], at_z[(z + 15) % 16]) for z in range(16)]
    back_left = lax.ppermute(left, ("zl", T), z_up)
    on_right = lax.ppermute(right, ("zl", T), z_down)
    back_right = lax.ppermute(right, ("zl", T), z_up)
    on_left = lax.ppermute(left, ("zl", T), z_down)
    far_left = lax.ppermute(back_left, ("zl", T), z_up)
    far_right = lax.ppermute(on_right, ("zl", T), z_down)
    tokens = jnp.stack(
        [
            jnp.concatenate([left, back_left, far_left, on_left]),
            jnp.concatenate([right, back_right, far_right, on_right]),
        ]
    )
    outgoing = lax.dot_general(
        dispatch, tokens, (((2,), (1,)), ((0,), (0,))), preferred_element_type=F32
    ).astype(BF)
    mine = lax.all_to_all(
        outgoing.reshape(2 * LAYER_ROWS, D // 2), LAYER, split_axis=0, concat_axis=0, tiled=True
    )
    theirs = other_core(mine)
    gate_part = rows_by(gate_mine, mine) + rows_by(gate_other, theirs)
    up_part = rows_by(up_mine, mine) + rows_by(up_other, theirs)
    own = (jax.nn.silu(gate_part) * up_part).astype(BF)

    below = lax.ppermute(own, T, UP)
    above = lax.ppermute(own, T, DOWN)
    far_first = lax.ppermute(below[:88], T, UP)
    far_second = lax.ppermute(above[88:], T, DOWN)

    def out_of(pieces, at):
        rows = jnp.concatenate(pieces, axis=0)
        return lax.dot_general(
            rows, down_around[at : at + rows.shape[0]], (((0,), (0,)), ((), ())),
            preferred_element_type=F32,
        )

    half_out = (out_of([own, below, above], 0) + out_of([far_first, far_second], 528)).astype(BF)
    keep = lax.dynamic_slice_in_dim(half_out, core * 256, 256, 1)
    give = lax.dynamic_slice_in_dim(half_out, (1 - core) * 256, 256, 1)
    both = (keep.astype(F32) + other_core(give).astype(F32)).astype(BF)
    returned = lax.all_to_all(both, LAYER, split_axis=0, concat_axis=0, tiled=True)
    partial = lax.dot_general(
        combine,
        returned.reshape(2, LAYER_ROWS, 256),
        (((1,), (1,)), ((0,), (0,))),
        preferred_element_type=F32,
    ).reshape(2, 4, TOK, 256)
    sums = partial[:, 0]
    for s in range(1, 4):
        sent = partial[:, s].astype(BF)
        sums = sums + lax.ppermute(sent, "zl", [(j, (j - s) % 4) for j in range(4)]).astype(F32)
    result = mixed_cols.astype(F32)
    hidden_out = (result + jnp.concatenate([sums[0], sums[1]], axis=1)).astype(BF)
    return (hidden_out, expand_block, output_block, cache_cols)


def solution(mesh):
    fine = Mesh(mesh.devices.reshape(4, 4, 4, 2, 4), DP + (T,))
    rows_both = P(DP + (T,), None)
    in_specs = (
        P(DP, T),
        P(DP, None),
        P(DP, None),
        P(DP, None),
        P(),
        P(),
        P(),
        rows_both,
        rows_both,
        rows_both,
        rows_both,
        P(DP, None, T),
        P(DP, None, T),
        P(DP, None, T),
    )
    out_specs = (P(DP, T), P(None, T), P(None, T), P(DP, T))
    return jax.shard_map(body, mesh=fine, in_specs=in_specs, out_specs=out_specs, check_vma=False)
```
